512 devices in a mesh: group: 8 (over x, core), dom: 64 (over y, z).
Axes of the slice: x: 4, y: 4, z: 16, core: 2. Of those that a mesh axis runs over, the one named last changes fastest.
Arguments:
- density_modes: float32 [64, 65536], P(None, ('group', 'dom')), may hold values from -4 to 4, as said below
- wave_speed: float32 [65536], P(('group', 'dom')), may hold values from 0.5 to 8
- shock_flags: int32 [65536], P(('group', 'dom')), may hold values 0 or 1
- elem_mass: float32 [65536], P(('group', 'dom')), may hold values from 0.2 to 1
- stiff_eigs: float32 [64], replicated, may hold values from 0.1 to 20
- coupling: bfloat16 [64, 96, 65536], P(None, None, ('group', 'dom')), may hold values from -3 to 3
- interior_res: float32 [5, 64, 65536], P(None, None, ('group', 'dom')), may hold values from -6 to 6
- face_res: float32 [5, 96, 65536], P(None, None, ('group', 'dom')), may hold values from -6 to 6
- send_rows: int32 [786432], P(('group', 'dom')), may hold values from 0 to 768, as said below
- face_rows: int32 [2, 393216], P(None, ('group', 'dom')), may hold values from 0 to 1536, as said below
Outputs:
- elem_update: float32 [5, 64, 65536], P(None, None, ('group', 'dom'))
- slot_traces: float32 [5, 96, 65536], P(None, None, ('group', 'dom'))
The draws below stay inside these ranges and needn't reach their ends.
Inputs may be any that keep to these rules, and one draw needn't show every extreme that they name: `density_modes`: mode coefficients of each element fall with polynomial degree at an element's own rate. `send_rows`: A device's block lists, at position q * 24 + i, the slot it sends as the i-th to the device of dom index q in its own group, or 768 for an empty position. Every slot appears exactly once. At most 24 slots go from one device to one owner, and in every group two owners receive 24 from every device of the group. `face_rows`: each received row that carries a slot is named exactly once in its device's block; unused faces hold 1536 in both entries; in every group some device uses all 768 faces.
All inputs are finite; a program needn't handle non-finite values. No bound on the sum of `shock_flags` on one device may be relied on, other than what follows from the above.
Results may differ from the reference program's by a relative error of at most 0.0003.
Values sent between devices are 32-bit elements; how exact they have to be, the bound alone decides.
A program may use at most 64 MiB of HBM per device.

```python
import math
import jax
import jax.numpy as jnp
from jax import lax

ELEM_DEV = 128
MODES = 64
FNODES = 16
COMPS = 5
EFACES = 6
TRACE = 96
SLOTS = 768
CAP = 24
ROWS = 1536
FACES = 768
ELEMS = 65536
N_GROUP = 8
N_DOM = 64


def draw_density_modes(key, part):
    mode_ids = jnp.arange(MODES, dtype=jnp.int32)
    degree = jnp.maximum(jnp.maximum(mode_ids // 16, mode_ids // 4 % 4), mode_ids % 4).astype(jnp.float32)
    decay_rates = jax.random.uniform(jax.random.fold_in(key, 1), (ELEMS,), jnp.float32, 0.0, 1.2)
    values = jax.random.truncated_normal(jax.random.fold_in(key, 2), -4.0, 4.0, (MODES, ELEMS), jnp.float32)
    return values * jnp.power(10.0, -decay_rates[None, :] * degree[:, None])


def draw_wave_speed(key, part):
    top_speed = jax.random.uniform(jax.random.fold_in(key, 21), (), jnp.float32, 2.0, 8.0)
    fraction = jax.random.uniform(jax.random.fold_in(key, 22), (ELEMS,), jnp.float32, 0.0, 1.0)
    base = 0.5 * jnp.exp(fraction * jnp.log(0.5 * top_speed))
    peak_ids = jax.random.randint(jax.random.fold_in(key, 23), (4,), 0, ELEMS, dtype=jnp.int32)
    element_ids = jnp.arange(ELEMS, dtype=jnp.int32)
    peaked = jnp.any(element_ids[:, None] == peak_ids[None, :], axis=1)
    return jnp.where(peaked, top_speed, base).astype(jnp.float32)


def route_tables(key):
    dom_size = N_DOM
    slot_total = SLOTS
    capacity = CAP
    row_total = ROWS
    spread = slot_total - 2 * capacity
    base_load = spread // (dom_size - 2)
    extra_count = spread % (dom_size - 2)
    owners = jnp.arange(dom_size, dtype=jnp.int32)
    profile = jnp.where(owners < 2, capacity, base_load + (owners - 2 < extra_count).astype(jnp.int32)).astype(jnp.int32)
    group_ids = jnp.arange(N_GROUP, dtype=jnp.int32)
    load_key = jax.random.fold_in(key, 11)
    owner_loads = jax.vmap(lambda group_index: profile[jax.random.permutation(jax.random.fold_in(load_key, group_index), dom_size)])(group_ids)
    load_ends = jnp.cumsum(owner_loads, axis=1).astype(jnp.int32)
    starts = load_ends - owner_loads
    tickets = jnp.arange(slot_total, dtype=jnp.int32)
    send_key = jax.random.fold_in(key, 12)

    def sender(device_index, ends_group, starts_group):
        shuffled = jax.random.permutation(jax.random.fold_in(send_key, device_index), slot_total).astype(jnp.int32)
        target = jnp.sum((ends_group[None, :] <= tickets[:, None]).astype(jnp.int32), axis=1)
        within = tickets - starts_group[target]
        placed = target * capacity + within
        return jnp.full((row_total,), slot_total, jnp.int32).at[placed].set(shuffled)
    sends = jax.vmap(lambda group_index: jax.vmap(lambda dom_index: sender(group_index * dom_size + dom_index, load_ends[group_index], starts[group_index]))(owners))(group_ids)
    row_ids = jnp.arange(row_total, dtype=jnp.int32)
    face_ids = jnp.arange(FACES, dtype=jnp.int32)
    recv_key = jax.random.fold_in(key, 13)

    def receiver(device_index, owner_load):
        usable = row_ids % capacity < owner_load
        jitter = jax.random.randint(jax.random.fold_in(recv_key, device_index), (row_total,), 0, 4096, dtype=jnp.int32)
        scores = jnp.where(usable, jitter * row_total + row_ids, 4096 * row_total + row_ids)
        ranking = jnp.argsort(scores, stable=True).astype(jnp.int32)
        in_use = dom_size * owner_load
        first_row = jnp.where(2 * face_ids < in_use, ranking[2 * face_ids], row_total)
        second = jnp.where(2 * face_ids < in_use, ranking[2 * face_ids + 1], row_total)
        return jnp.stack([first_row, second])
    recvs = jax.vmap(lambda group_index: jax.vmap(lambda dom_index: receiver(group_index * dom_size + dom_index, owner_loads[group_index, dom_index]))(owners))(group_ids)
    send_flat = sends.reshape(-1)
    face_flat = jnp.transpose(recvs, (2, 0, 1, 3)).reshape(2, -1)
    return (send_flat, face_flat)


def draw_send_rows(key, part):
    return route_tables(key)[0]


def draw_face_rows(key, part):
    return route_tables(key)[1]


def plant(entries, key, least, largest):
    place = [jax.random.randint(jax.random.fold_in(key, axis), (), 0, length) for axis, length in enumerate(entries.shape)]
    longest = entries.shape.index(max(entries.shape))
    neighbour = place[:longest] + [(place[longest] + 1) % entries.shape[longest]] + place[longest + 1:]
    return entries.at[tuple(place)].set(least).at[tuple(neighbour)].set(largest)


def shard_levels(key, dims, cuts, least, largest):
    factor_of, own = 1.0, jax.random.fold_in(key, 6)
    for dim, parts in cuts:
        steps = jnp.exp(jax.random.uniform(jax.random.fold_in(own, dim), (parts,), jnp.float32, least / len(cuts), largest / len(cuts)))
        factor_of = factor_of * jnp.repeat(steps, dims[dim] // parts).reshape([-1 if axis == dim else 1 for axis in range(len(dims))])
    return factor_of


def bell_draw(rng, shape, scale, reach, shards=(), kind=jnp.bfloat16):
    drawn = jax.random.normal(rng, shape, jnp.float32) * scale
    if len(shards) > 0:
        drawn = shard_levels(rng, shape, shards, -0.22, 0.18) * drawn
    return jnp.clip(drawn, min=-reach, max=reach).astype(kind)


def setup_inputs(seed: int = 0) -> dict:
    key_list = jax.random.split(jax.random.key(seed), 11)
    density_modes = draw_density_modes(jax.random.fold_in(key_list[10], 71), 0)
    wave_speed = draw_wave_speed(jax.random.fold_in(key_list[10], 71), 0)
    shock_flags = plant((jax.random.randint(key_list[2], (ELEMS,), 0, 8) < 1).astype(jnp.int32), jax.random.fold_in(key_list[2], 1), 0, 1)
    elem_mass = jnp.clip(jnp.exp(math.log(1.0) - 1.609438 * jax.random.uniform(key_list[3], (ELEMS,), jnp.float32) ** shard_levels(key_list[3], (ELEMS,), ((0, 512),), -0.2, 0.2)), 0.2, 1.0)
    stiff_eigs = jnp.clip(jnp.exp(jax.random.uniform(key_list[4], (MODES,), jnp.float32, math.log(0.1), math.log(20.0))), 0.1, 20.0)
    coupling = bell_draw(key_list[5], (MODES, TRACE, ELEMS), 0.5, 3.0, ((2, 512),))
    interior_res = bell_draw(key_list[6], (COMPS, MODES, ELEMS), 1.0, 6.0, ((2, 512),), jnp.float32)
    face_res = bell_draw(key_list[7], (COMPS, TRACE, ELEMS), 1.0, 6.0, ((2, 512),), jnp.float32)
    send_rows = draw_send_rows(jax.random.fold_in(key_list[10], 71), 0)
    face_rows = draw_face_rows(jax.random.fold_in(key_list[10], 71), 0)
    return {"density_modes": density_modes, "wave_speed": wave_speed, "shock_flags": shock_flags, "elem_mass": elem_mass, "stiff_eigs": stiff_eigs, "coupling": coupling, "interior_res": interior_res, "face_res": face_res, "send_rows": send_rows, "face_rows": face_rows}


EPS_SCALE = 0.1
NU_BASE = 0.02
TAU_STAB = 1.0
SENSOR_MID = -2.0
SENSOR_WIDTH = 0.5
RATIO_FLOOR = 0.0001

def sensor_visc(density_modes, wave_speed, shock_flags):
    mode_ids = jnp.arange(MODES, dtype=jnp.int32)
    degree = jnp.maximum(jnp.maximum(mode_ids // 16, mode_ids // 4 % 4), mode_ids % 4)
    top_mask = (degree == 3).astype(jnp.float32)
    squares = density_modes * density_modes
    totals = jnp.sum(squares, axis=0) + 1e-06
    high_part = jnp.sum(squares * top_mask[:, None], axis=0)
    sensor = jnp.log10(jnp.maximum(high_part / totals, RATIO_FLOOR))
    ramped = 0.5 * (1.0 + jnp.tanh((sensor - SENSOR_MID) / SENSOR_WIDTH))
    return EPS_SCALE * wave_speed * jnp.maximum(ramped, 0.5 * shock_flags.astype(jnp.float32))

def element_terms(coupling, c_coef, interior_res, face_res):
    widened = coupling.astype(jnp.float32)
    scaled = widened * c_coef[:, None, :]
    width_n = widened.shape[2]
    shaped_full = widened.reshape(MODES, EFACES, FNODES, width_n)
    shaped_scaled = scaled.reshape(MODES, EFACES, FNODES, width_n)
    blocks = jnp.einsum('kjan,kjbn->jabn', shaped_scaled, shaped_full, precision=lax.Precision.HIGHEST)
    blocks = blocks + TAU_STAB * jnp.eye(FNODES, dtype=jnp.float32)[None, :, :, None]
    weighted = c_coef[None, :, :] * interior_res
    loads = face_res - jnp.einsum('ktn,ckn->ctn', widened, weighted, precision=lax.Precision.HIGHEST)
    return (blocks, loads)

def back_substitute(coupling, c_coef, interior_res, traces):
    widened = coupling.astype(jnp.float32)
    pulled = jnp.einsum('kte,cte->cke', widened, traces, precision=lax.Precision.HIGHEST)
    return c_coef[None, :, :] * (interior_res - pulled)

def reference(density_modes, wave_speed, shock_flags, elem_mass, stiff_eigs, coupling, interior_res, face_res, send_rows, face_rows):
    peak = jnp.max(wave_speed)
    viscous = sensor_visc(density_modes, wave_speed, shock_flags)
    dom_size = N_DOM
    per_group = dom_size * ELEM_DEV
    slot_group = dom_size * SLOTS

    def one_group(group_index):
        start = (group_index * per_group).astype(jnp.int32)

        def cut(array):
            return lax.dynamic_slice_in_dim(array, start, per_group, axis=array.ndim - 1)
        eps_group = cut(viscous)
        speed_group = cut(wave_speed)
        mass_group = cut(elem_mass)
        coupling_group = cut(coupling)
        inner_group = cut(interior_res)
        faceres_group = cut(face_res)
        send_group = lax.dynamic_slice_in_dim(send_rows, (group_index * dom_size * ROWS).astype(jnp.int32), dom_size * ROWS, axis=0).reshape(dom_size, ROWS)
        rows_group = lax.dynamic_slice_in_dim(face_rows, (group_index * dom_size * FACES).astype(jnp.int32), dom_size * FACES, axis=1).reshape(2, dom_size, FACES)
        usable = rows_group < ROWS
        clipped = jnp.minimum(rows_group, ROWS - 1)
        source = clipped // CAP
        offset = clipped % CAP
        owner = jnp.arange(dom_size, dtype=jnp.int32)[None, :, None]
        slot_ids = send_group[source, owner * CAP + offset] + source * SLOTS
        slot_first = jnp.minimum(slot_ids[0].reshape(-1), slot_group - 1)
        slot_second = jnp.minimum(slot_ids[1].reshape(-1), slot_group - 1)
        face_ok = usable[0].reshape(-1)
        drop_first = jnp.where(face_ok, slot_first, slot_group)
        drop_second = jnp.where(face_ok, slot_second, slot_group)
        eps_slots = jnp.tile(eps_group.reshape(dom_size, 1, ELEM_DEV), (1, EFACES, 1)).reshape(slot_group)
        face_visc = 0.5 * (eps_slots[slot_first] + eps_slots[slot_second])
        slot_visc = jnp.zeros((slot_group,), jnp.float32).at[drop_first].set(face_visc, mode='drop').at[drop_second].set(face_visc, mode='drop')
        nu_elem = NU_BASE + jnp.mean(slot_visc.reshape(dom_size, EFACES, ELEM_DEV), axis=1).reshape(per_group)
        c_coef = 1.0 / (mass_group[None, :] * (1.0 + speed_group[None, :] / peak + nu_elem[None, :] * stiff_eigs[:, None]))
        blocks, loads = element_terms(coupling_group, c_coef, inner_group, faceres_group)
        slot_blocks = blocks.reshape(EFACES, FNODES, FNODES, dom_size, ELEM_DEV).transpose(3, 0, 4, 1, 2).reshape(slot_group, FNODES, FNODES)
        slot_loads = loads.reshape(COMPS, EFACES, FNODES, dom_size, ELEM_DEV).transpose(3, 1, 4, 0, 2).reshape(slot_group, COMPS, FNODES)
        face_mask = face_ok[:, None, None]
        face_block = jnp.where(face_mask, slot_blocks[slot_first] + slot_blocks[slot_second], jnp.eye(FNODES, dtype=jnp.float32)[None, :, :])
        face_load = jnp.where(face_mask, slot_loads[slot_first] + slot_loads[slot_second], 0.0)
        face_trace = jnp.linalg.solve(face_block, jnp.transpose(face_load, (0, 2, 1))).transpose(0, 2, 1)
        slot_trace = jnp.zeros((slot_group, COMPS, FNODES), jnp.float32).at[drop_first].set(face_trace, mode='drop').at[drop_second].set(face_trace, mode='drop')
        traces = slot_trace.reshape(dom_size, EFACES, ELEM_DEV, COMPS, FNODES).transpose(3, 1, 4, 0, 2).reshape(COMPS, EFACES * FNODES, per_group)
        update = back_substitute(coupling_group, c_coef, inner_group, traces)
        return (update, traces)
    updates, traces_all = lax.map(one_group, jnp.arange(N_GROUP, dtype=jnp.int32))
    elem_update = jnp.transpose(updates, (1, 2, 0, 3)).reshape(COMPS, MODES, ELEMS)
    slot_traces = jnp.transpose(traces_all, (1, 2, 0, 3)).reshape(COMPS, TRACE, ELEMS)
    return (elem_update, slot_traces)
```

```python
import functools

import jax
import jax.numpy as jnp
from jax import lax
from jax.experimental import pallas as pl
from jax.experimental.pallas import tpu as pltpu
from jax.sharding import PartitionSpec as P

MODES = 64
FNODES = 16
COMPS = 5
EFACES = 6
TRACE = 96
ELEM_DEV = 128
SLOTS = EFACES * ELEM_DEV
CAP = 24
N_DOM = 64
N_GROUP = 8
ROWS = N_DOM * CAP
FACES = 768
TRI = 136
WIDE = 256
LANES = 128
OUT_TILE = 40
RET_TILE = 16

EPS_SCALE = 0.1
NU_BASE = 0.02
TAU_STAB = 1.0
SENSOR_MID = -2.0
SENSOR_WIDTH = 0.5
RATIO_FLOOR = 0.0001

F32 = jnp.float32
BF16 = jnp.bfloat16
I32 = jnp.int32
MESH = pl.DeviceIdType.MESH
NN = (((1,), (0,)), ((), ()))
NT = (((1,), (1,)), ((), ()))
VMEM_LIMIT = 60 * 1024 * 1024


def iota(shape, axis):
    return lax.broadcasted_iota(I32, shape, axis)


def split3(x):
    high = x.astype(BF16)
    rest = x - high.astype(F32)
    middle = rest.astype(BF16)
    low = (rest - middle.astype(F32)).astype(BF16)
    return high, middle, low


def split2(x):
    high = x.astype(BF16)
    return high, (x - high.astype(F32)).astype(BF16)


def dot(a, b, dims):
    return lax.dot_general(a, b, dims, preferred_element_type=F32)


def one_hot(mask):
    return jnp.where(mask, 1.0, 0.0).astype(BF16)


def element_eps(density, speed, flags):
    ids = iota((MODES, LANES), 0)
    degree = jnp.maximum(jnp.maximum(ids >> 4, (ids >> 2) & 3), ids & 3)
    squares = density * density
    totals = jnp.sum(squares, axis=0, keepdims=True) + 1e-06
    high = jnp.sum(jnp.where(degree == 3, squares, 0.0), axis=0, keepdims=True)
    sensor = jnp.log10(jnp.maximum(high / totals, RATIO_FLOOR))
    ramped = 0.5 * (1.0 + jnp.tanh((sensor - SENSOR_MID) / SENSOR_WIDTH))
    return EPS_SCALE * speed * jnp.maximum(ramped, 0.5 * flags.astype(F32))


def padded_row(row):
    source = (row * 2731) >> 16
    return source, row - source * CAP


def partner_rows(face_ref, fcol_ref):
    high_parts = []
    low_parts = []
    for end in range(2):
        own_p, own_i = padded_row(face_ref[end : end + 1, :])
        other_p, other_i = padded_row(face_ref[1 - end : 2 - end, :])
        mine = iota((16, FACES), 0) == (own_p >> 2)
        high_parts.append(
            jnp.concatenate(
                [
                    jnp.where(mine, other_p.astype(F32), 0.0),
                    jnp.where(mine, other_i.astype(F32), 0.0),
                ],
                axis=0,
            ).astype(BF16)
        )
        columns = []
        for chunk in range(6):
            col_p, col_i = padded_row(fcol_ref[:, end * 6 + chunk : end * 6 + chunk + 1])
            place = ((col_p & 3) << 5) + col_i
            columns.append(one_hot(iota((LANES, LANES), 1) == place))
        low_parts.append(jnp.concatenate(columns, axis=0))
    found = dot(high_parts[0], low_parts[0], NN) + dot(high_parts[1], low_parts[1], NN)
    found = found.astype(I32)
    return found[0:16], found[16:32]


def remote(src, dst, send_sem, recv_sem, where):
    return pltpu.make_async_remote_copy(
        src_ref=src,
        dst_ref=dst,
        send_sem=send_sem,
        recv_sem=recv_sem,
        device_id=where,
        device_id_type=MESH,
    )


def coef_kernel(
    density_ref,
    speed_ref,
    flags_ref,
    mass_ref,
    eigs_ref,
    send_ref,
    face_ref,
    fcol_ref,
    coef_ref,
    outgoing,
    arrived,
    returning,
    back,
    top_out,
    tops,
    send_a,
    recv_a,
    send_b,
    recv_b,
    send_c,
    recv_c,
):
    me = lax.axis_index("dom")
    group = lax.axis_index("group")
    barrier = pltpu.get_barrier_semaphore()

    def greet(k, carry):
        pl.semaphore_signal(
            barrier, inc=1, device_id={"dom": lax.rem(me + k, N_DOM)}, device_id_type=MESH
        )
        return carry

    lax.fori_loop(1, N_DOM, greet, 0)

    def greet_group(k, carry):
        pl.semaphore_signal(
            barrier, inc=1, device_id={"group": lax.rem(group + k, N_GROUP)}, device_id_type=MESH
        )
        return carry

    lax.fori_loop(1, N_GROUP, greet_group, 0)

    speed = speed_ref[...]
    eps = element_eps(density_ref[...], speed, flags_ref[...])
    slots = send_ref[...]
    lane = iota((N_DOM, LANES), 1)
    values = jnp.take_along_axis(
        jnp.broadcast_to(eps, (N_DOM, LANES)), slots & (ELEM_DEV - 1), axis=1
    )
    values = jnp.where(slots < SLOTS, values, 0.0)
    values = jnp.where(lane == LANES - 1, jnp.max(speed, axis=1, keepdims=True), values)
    for q in range(N_DOM):
        outgoing[q] = values[q : q + 1, :]

    pl.semaphore_wait(barrier, N_DOM + N_GROUP - 2)

    def send_first(k, carry):
        q = lax.rem(me + k, N_DOM)
        remote(outgoing.at[q], arrived.at[me], send_a, recv_a, {"dom": q}).start()
        return carry

    lax.fori_loop(1, N_DOM, send_first, 0)
    arrived[me] = outgoing[me]
    partner_p, partner_i = partner_rows(face_ref, fcol_ref)
    others = pl.ds(0, N_DOM - 1)
    whole = remote(outgoing.at[others], arrived.at[others], send_a, recv_a, {"dom": lax.rem(me + 1, N_DOM)})
    whole.wait_recv()
    whole.wait_send()

    partner_eps = jnp.zeros((16, LANES), F32)
    top = jnp.zeros((1, LANES), F32)
    for p in range(N_DOM):
        row = arrived[p]
        top = jnp.maximum(top, row)
        found = jnp.take_along_axis(jnp.broadcast_to(row, (16, LANES)), partner_i, axis=1)
        partner_eps = jnp.where(partner_p == p, found, partner_eps)
    for r in range(16):
        returning[r] = partner_eps[r : r + 1, :]
    top_out[0] = top

    def send_second(k, carry):
        p = lax.rem(me + k, N_DOM)
        remote(returning.at[lax.div(p, 4)], back.at[me], send_b, recv_b, {"dom": p}).start()
        return carry

    lax.fori_loop(1, N_DOM, send_second, 0)

    def send_top(k, carry):
        other = lax.rem(group + k, N_GROUP)
        remote(top_out.at[0], tops.at[group], send_c, recv_c, {"group": other}).start()
        return carry

    lax.fori_loop(1, N_GROUP, send_top, 0)
    back[me] = returning[lax.div(me, 4)]
    tops[group] = top_out[0]

    whole = remote(arrived.at[others], back.at[others], send_b, recv_b, {"dom": lax.rem(me + 1, N_DOM)})
    whole.wait_recv()
    whole.wait_send()
    seven = pl.ds(0, N_GROUP - 1)
    whole = remote(tops.at[seven], tops.at[seven], send_c, recv_c, {"group": lax.rem(group + 1, N_GROUP)})
    whole.wait_recv()
    whole.wait_send()

    rows = jnp.concatenate([back[q] for q in range(N_DOM)], axis=0)
    rows = pltpu.roll(rows, lax.rem(4 - lax.rem(me, 4), 4) * 32, 1)
    total = jnp.zeros((N_DOM, LANES), F32)
    for i in range(CAP):
        slot = slots[:, i : i + 1]
        here = jnp.logical_and((slot & (ELEM_DEV - 1)) == lane, slot < SLOTS)
        total = total + jnp.where(here, rows[:, i : i + 1], 0.0)
    gathered = jnp.sum(total, axis=0, keepdims=True)
    nu = NU_BASE + (EFACES * eps + gathered) / (2.0 * EFACES)
    top = tops[0]
    for g in range(1, N_GROUP):
        top = jnp.maximum(top, tops[g])
    lane_one = iota((1, LANES), 1)
    peak = jnp.max(jnp.where(lane_one == LANES - 1, top, 0.0), axis=1, keepdims=True)
    coef_ref[...] = 1.0 / (mass_ref[...] * (1.0 + speed / peak + nu * eigs_ref[...]))


def coefficients(density, speed, flags, mass, eigs, send64, face_rows, fcols):
    vmem = pl.BlockSpec(memory_space=pltpu.VMEM)
    return pl.pallas_call(
        coef_kernel,
        out_shape=jax.ShapeDtypeStruct((MODES, LANES), F32),
        in_specs=[vmem] * 8,
        out_specs=vmem,
        scratch_shapes=[
            pltpu.VMEM((N_DOM, 1, LANES), F32),
            pltpu.VMEM((N_DOM, 1, LANES), F32),
            pltpu.VMEM((16, 1, LANES), F32),
            pltpu.VMEM((N_DOM, 1, LANES), F32),
            pltpu.VMEM((1, 1, LANES), F32),
            pltpu.VMEM((N_GROUP, 1, LANES), F32),
        ]
        + [pltpu.SemaphoreType.DMA] * 6,
        compiler_params=pltpu.CompilerParams(collective_id=0, has_side_effects=True),
        name="coefficients",
    )(density, speed, flags, mass, eigs, send64, face_rows, fcols)


def block_kernel(coef_ref, coupling_ref, inner_ref, face_ref, scol_ref, out_ref, tail_ref, pay, rows):
    for j in range(EFACES):
        def body(k, sums):
            coef = coef_ref[pl.ds(k, 1), :]
            c = coupling_ref[k, j * FNODES : (j + 1) * FNODES, :].astype(F32)
            u = c * coef
            new = [sums[0] + u * c]
            for d in range(1, 8):
                new.append(sums[d] + u * pltpu.roll(c, FNODES - d, 0))
            new.append(sums[8] + u[0:8] * c[8:16])
            for comp in range(COMPS):
                new.append(sums[9 + comp] + c * (coef * inner_ref[comp, pl.ds(k, 1), :]))
            return tuple(new)

        full = jnp.zeros((FNODES, LANES), F32)
        start = (full + TAU_STAB,) + (full,) * 7 + (jnp.zeros((8, LANES), F32),) + (full,) * COMPS
        sums = lax.fori_loop(0, MODES, body, start, unroll=2)
        at = pl.ds(j * LANES, LANES)
        for d in range(9):
            height = 16 if d < 8 else 8
            pay[pl.ds(d * 16, height), at] = sums[d]
        for comp in range(COMPS):
            pay[pl.ds(TRI + comp * FNODES, FNODES), at] = (
                face_ref[comp, j * FNODES : (j + 1) * FNODES, :] - sums[9 + comp]
            )
        pay[pl.ds(216, WIDE - 216), at] = jnp.zeros((WIDE - 216, LANES), F32)

    parts = split3(pay[...])
    lane = iota((8, LANES), 1)
    sub = iota((8, LANES), 0)
    for chunk in range(4):
        hot = one_hot(iota((384, SLOTS), 1) == scol_ref[:, chunk : chunk + 1])
        rows[...] = dot(hot, parts[0], NT) + dot(hot, parts[1], NT) + dot(hot, parts[2], NT)

        def pack(n, carry):
            q = chunk * 16 + n
            base = pl.multiple_of(n * CAP, 8)
            out_ref[q, 0:CAP, :] = rows[pl.ds(base, CAP), 0:LANES]
            x0 = rows[pl.ds(base, 8), LANES:WIDE]
            x1 = rows[pl.ds(base + 8, 8), LANES:WIDE]
            x2 = rows[pl.ds(base + 16, 8), LANES:WIDE]
            out_ref[q, CAP : CAP + 8, :] = jnp.where(lane < 64, x0, pltpu.roll(x1, 64, 1))
            out_ref[q, CAP + 8 : CAP + 16, :] = jnp.where(
                lane < 64,
                x2,
                jnp.where(
                    lane < 88,
                    x0,
                    jnp.where(lane < 112, pltpu.roll(x1, 24, 1), pltpu.roll(x2, 48, 1)),
                ),
            )
            spread = pltpu.roll(x2, 48, 1, stride=8, stride_axis=0)
            tail_ref[q] = jnp.sum(jnp.where((lane >> 3) == sub, spread, 0.0), axis=0, keepdims=True)
            return carry

        lax.fori_loop(0, 16, pack, 0)


def blocks_packed(coef, coupling, inner, face_res, scol):
    vmem = pl.BlockSpec(memory_space=pltpu.VMEM)
    return pl.pallas_call(
        block_kernel,
        out_shape=(
            jax.ShapeDtypeStruct((N_DOM, OUT_TILE, LANES), F32),
            jax.ShapeDtypeStruct((N_DOM, 1, LANES), F32),
        ),
        in_specs=[vmem] * 5,
        out_specs=(vmem, vmem),
        scratch_shapes=[pltpu.VMEM((WIDE, SLOTS), F32), pltpu.VMEM((384, WIDE), F32)],
        compiler_params=pltpu.CompilerParams(vmem_limit_bytes=VMEM_LIMIT),
        name="blocks_packed",
    )(coef, coupling, inner, face_res, scol)


def exchange_kernel(count, *refs):
    sources = refs[:count]
    targets = refs[count : 2 * count]
    send_sem, recv_sem, own_sem = refs[2 * count :]
    me = lax.axis_index("dom")
    barrier = pltpu.get_barrier_semaphore()

    def greet(k, carry):
        pl.semaphore_signal(
            barrier, inc=1, device_id={"dom": lax.rem(me + k, N_DOM)}, device_id_type=MESH
        )
        return carry

    lax.fori_loop(1, N_DOM, greet, 0)
    own = [
        pltpu.make_async_copy(sources[n].at[me], targets[n].at[me], own_sem.at[n])
        for n in range(count)
    ]
    for copy in own:
        copy.start()
    pl.semaphore_wait(barrier, N_DOM - 1)

    def start(k, carry):
        q = lax.rem(me + k, N_DOM)
        for n in range(count):
            remote(
                sources[n].at[q], targets[n].at[me], send_sem.at[n], recv_sem.at[n], {"dom": q}
            ).start()
        return carry

    lax.fori_loop(1, N_DOM, start, 0)
    for copy in own:
        copy.wait()
    others = pl.ds(0, N_DOM - 1)
    for n in range(count):
        whole = remote(
            sources[n].at[others],
            targets[n].at[others],
            send_sem.at[n],
            recv_sem.at[n],
            {"dom": lax.rem(me + 1, N_DOM)},
        )
        whole.wait_recv()
        whole.wait_send()


def exchange(arrays, collective_id):
    anywhere = pl.BlockSpec(memory_space=pl.ANY)
    count = len(arrays)
    return pl.pallas_call(
        functools.partial(exchange_kernel, count),
        out_shape=tuple(jax.ShapeDtypeStruct(a.shape, a.dtype) for a in arrays),
        in_specs=[anywhere] * count,
        out_specs=(anywhere,) * count,
        scratch_shapes=[pltpu.SemaphoreType.DMA((count,))] * 3,
        compiler_params=pltpu.CompilerParams(collective_id=collective_id, has_side_effects=True),
        name=f"exchange_{collective_id}",
    )(*arrays)


def solve_faces(grid, idle):
    def entry(i, j):
        d = (j - i) % FNODES
        if d > 8 or (d == 8 and i >= 8):
            i, d = j, FNODES - d
        return grid(d * 16 + i)

    scaled = [[None] * FNODES for _ in range(FNODES)]
    lower = [[None] * FNODES for _ in range(FNODES)]
    inverse = [None] * FNODES
    for j in range(FNODES):
        for i in range(j, FNODES):
            total = entry(i, j)
            if i == j:
                total = total + idle
            for k in range(j):
                total = total - scaled[i][k] * lower[j][k]
            if i == j:
                inverse[j] = 1.0 / total
            else:
                scaled[i][j] = total
                lower[i][j] = total * inverse[j]
    solved = [[None] * FNODES for _ in range(COMPS)]
    for comp in range(COMPS):
        forward = []
        for i in range(FNODES):
            total = grid(TRI + comp * FNODES + i)
            for k in range(i):
                total = total - lower[i][k] * forward[k]
            forward.append(total)
        for i in reversed(range(FNODES)):
            total = forward[i] * inverse[i]
            for k in range(i + 1, FNODES):
                total = total - lower[k][i] * solved[comp][k]
            solved[comp][i] = total
    return solved


def solve_kernel(arrived_ref, tail_ref, face_ref, fcol_ref, idle_ref, ret_ref, part_a, part_b, part_c, grid, answer, rows):
    lane = iota((8, LANES), 1)
    sub = iota((8, LANES), 0)

    def unpack(p, carry):
        base = pl.multiple_of(p * CAP, 8)
        b = arrived_ref[p, CAP : CAP + 8, :]
        c = arrived_ref[p, CAP + 8 : CAP + 16, :]
        tail = jnp.broadcast_to(tail_ref[p], (8, LANES))
        spread = jnp.take_along_axis(
            pltpu.roll(tail, 24, 1, stride=8, stride_axis=0), 7 - sub, axis=0
        )
        zero = jnp.zeros((8, LANES), F32)
        x0 = jnp.where(lane < 64, b, jnp.where(lane < 88, c, zero))
        x1 = jnp.where(
            lane < 64, pltpu.roll(b, 64, 1), jnp.where(lane < 88, pltpu.roll(c, 104, 1), zero)
        )
        x2 = jnp.where(
            lane < 64,
            c,
            jnp.where(lane < 80, pltpu.roll(c, 80, 1), jnp.where(lane < 88, spread, zero)),
        )
        rows[pl.ds(base, CAP), 0:LANES] = arrived_ref[p, 0:CAP, :]
        rows[pl.ds(base, 8), LANES:WIDE] = x0
        rows[pl.ds(base + 8, 8), LANES:WIDE] = x1
        rows[pl.ds(base + 16, 8), LANES:WIDE] = x2
        return carry

    lax.fori_loop(0, N_DOM, unpack, 0, unroll=2)
    high, middle, low = split3(rows[...])
    part_a[...] = high
    part_b[...] = middle
    part_c[...] = low
    for chunk in range(6):
        first = fcol_ref[:, chunk : chunk + 1]
        second = fcol_ref[:, 6 + chunk : 7 + chunk]
        received = iota((LANES, ROWS), 1)
        hot = one_hot(jnp.logical_or(received == first, received == second))
        joined = (
            dot(hot, part_a[...], NN) + dot(hot, part_b[...], NN) + dot(hot, part_c[...], NN)
        )
        turned = jnp.transpose(joined)
        grid[pl.ds(chunk, 216, stride=8), :] = turned[0:216, :]

    solved = solve_faces(lambda n: grid[n * 8 : n * 8 + 8, :], idle_ref[...])
    for comp in range(COMPS):
        for i in range(FNODES):
            n = comp * FNODES + i
            answer[n * 8 : n * 8 + 8, :] = solved[comp][i]
    traces = jnp.concatenate(
        [answer[pl.ds(chunk, COMPS * FNODES, stride=8), :] for chunk in range(6)], axis=1
    )
    gap = jnp.zeros((LANES - COMPS * FNODES, FACES), BF16)
    high, low = split2(traces)
    both = jnp.concatenate([high, gap, low, gap], axis=0)
    for chunk in range(4):
        received = iota((384, FACES), 0) + chunk * 384
        hot = one_hot(
            jnp.logical_or(received == face_ref[0:1, :], received == face_ref[1:2, :])
        )
        found = dot(hot, both, NT)
        rows[pl.ds(chunk * 384, 384), 0:LANES] = found[:, 0:LANES] + found[:, LANES:WIDE]

    def pack(p, carry):
        base = pl.multiple_of(p * CAP, 8)
        y0 = rows[pl.ds(base, 8), 0:LANES]
        y1 = rows[pl.ds(base + 8, 8), 0:LANES]
        y2 = rows[pl.ds(base + 16, 8), 0:LANES]
        ret_ref[p, 0:8, :] = jnp.where(lane < 64, y0, pltpu.roll(y1, 64, 1))
        ret_ref[p, 8:16, :] = jnp.where(
            lane < 64,
            y2,
            jnp.where(
                lane < 80, y0, jnp.where(lane < 96, pltpu.roll(y1, 16, 1), pltpu.roll(y2, 32, 1))
            ),
        )
        return carry

    lax.fori_loop(0, N_DOM, pack, 0, unroll=2)


def face_traces(arrived, tails, face_rows, fcols, idle):
    vmem = pl.BlockSpec(memory_space=pltpu.VMEM)
    return pl.pallas_call(
        solve_kernel,
        out_shape=jax.ShapeDtypeStruct((N_DOM, RET_TILE, LANES), F32),
        in_specs=[vmem] * 5,
        out_specs=vmem,
        scratch_shapes=[
            pltpu.VMEM((ROWS, WIDE), BF16),
            pltpu.VMEM((ROWS, WIDE), BF16),
            pltpu.VMEM((ROWS, WIDE), BF16),
            pltpu.VMEM((216 * 8, LANES), F32),
            pltpu.VMEM((80 * 8, LANES), F32),
            pltpu.VMEM((ROWS, WIDE), F32),
        ],
        compiler_params=pltpu.CompilerParams(vmem_limit_bytes=VMEM_LIMIT),
        name="face_traces",
    )(arrived, tails, face_rows, fcols, idle)


def update_kernel(back_ref, srow_ref, coef_ref, coupling_ref, inner_ref, update_ref, traces_ref, parts):
    lane = iota((8, LANES), 1)

    def unpack(q, carry):
        base = pl.multiple_of(q * CAP, 8)
        b = back_ref[q, 0:8, :]
        c = back_ref[q, 8:16, :]
        zero = jnp.zeros((8, LANES), F32)
        y0 = jnp.where(lane < 64, b, jnp.where(lane < 80, c, zero))
        y1 = jnp.where(
            lane < 64, pltpu.roll(b, 64, 1), jnp.where(lane < 80, pltpu.roll(c, 112, 1), zero)
        )
        y2 = jnp.where(lane < 64, c, jnp.where(lane < 80, pltpu.roll(c, 96, 1), zero))
        parts[pl.ds(base, CAP), :] = jnp.concatenate([y0, y1, y2], axis=0)
        return carry

    lax.fori_loop(0, N_DOM, unpack, 0, unroll=2)
    high, low = split2(parts[...])
    both = jnp.concatenate([high, low], axis=1)
    for j in range(EFACES):
        slot = iota((LANES, ROWS), 0) + j * LANES
        hot = one_hot(slot == srow_ref[...])
        found = dot(hot, both, NN)
        turned = jnp.transpose(found[:, 0:LANES] + found[:, LANES:WIDE])
        for comp in range(COMPS):
            traces_ref[comp, j * FNODES : (j + 1) * FNODES, :] = turned[
                comp * FNODES : (comp + 1) * FNODES, :
            ]

    def body(k, carry):
        c = coupling_ref[k].astype(F32)
        coef = coef_ref[pl.ds(k, 1), :]
        for comp in range(COMPS):
            pulled = jnp.sum(c * traces_ref[comp], axis=0, keepdims=True)
            update_ref[comp, pl.ds(k, 1), :] = coef * (inner_ref[comp, pl.ds(k, 1), :] - pulled)
        return carry

    lax.fori_loop(0, MODES, body, 0, unroll=2)


def back_substitute(back, srow, coef, coupling, inner):
    vmem = pl.BlockSpec(memory_space=pltpu.VMEM)
    return pl.pallas_call(
        update_kernel,
        out_shape=(
            jax.ShapeDtypeStruct((COMPS, MODES, LANES), F32),
            jax.ShapeDtypeStruct((COMPS, TRACE, LANES), F32),
        ),
        in_specs=[vmem] * 5,
        out_specs=(vmem, vmem),
        scratch_shapes=[pltpu.VMEM((ROWS, LANES), F32)],
        compiler_params=pltpu.CompilerParams(vmem_limit_bytes=VMEM_LIMIT),
        name="back_substitute",
    )(back, srow, coef, coupling, inner)


def local(
    density_modes,
    wave_speed,
    shock_flags,
    elem_mass,
    stiff_eigs,
    coupling,
    interior_res,
    face_res,
    send_rows,
    face_rows,
):
    send64 = jnp.pad(
        send_rows.reshape(N_DOM, CAP), ((0, 0), (0, LANES - CAP)), constant_values=SLOTS
    )
    scol = send_rows.reshape(4, 384).T
    fcols = face_rows.reshape(12, LANES).T
    idle = jnp.where(
        jnp.concatenate(
            [face_rows[0].reshape(6, LANES), jnp.full((2, LANES), ROWS, I32)], axis=0
        )
        < ROWS,
        0.0,
        1.0,
    ).astype(F32)
    coef = coefficients(
        density_modes,
        wave_speed[None, :],
        shock_flags[None, :],
        elem_mass[None, :],
        stiff_eigs[:, None],
        send64,
        face_rows,
        fcols,
    )
    packed, tails = blocks_packed(coef, coupling, interior_res, face_res, scol)
    arrived, arrived_tails = exchange((packed, tails), 1)
    returning = face_traces(arrived, arrived_tails, face_rows, fcols, idle)
    (back,) = exchange((returning,), 2)
    return back_substitute(back, send_rows[None, :], coef, coupling, interior_res)


def solution(mesh):
    return jax.shard_map(
        local,
        mesh=mesh,
        in_specs=(
            P(None, ("group", "dom")),
            P(("group", "dom")),
            P(("group", "dom")),
            P(("group", "dom")),
            P(),
            P(None, None, ("group", "dom")),
            P(None, None, ("group", "dom")),
            P(None, None, ("group", "dom")),
            P(("group", "dom")),
            P(None, ("group", "dom")),
        ),
        out_specs=(P(None, None, ("group", "dom")), P(None, None, ("group", "dom"))),
        check_vma=False,
    )
```

```python
import jax
import jax.numpy as jnp
from jax import lax
from jax.experimental import pallas as pl
from jax.experimental.pallas import tpu as pltpu
from jax.sharding import PartitionSpec as P

MODES = 64
FNODES = 16
COMPS = 5
EFACES = 6
TRACE = 96
ELEM_DEV = 128
SLOTS = EFACES * ELEM_DEV
CAP = 24
N_DOM = 64
N_GROUP = 8
ROWS = N_DOM * CAP
FACES = 768
TRI = 136
USED = 216
HEIGHT = 224
WIDE = 256
N_Z = 16
N_Y = N_DOM // N_Z
PART = N_Z * CAP
LANES = 128
OUT_TILE = 40
RET_TILE = 16

EPS_SCALE = 0.1
NU_BASE = 0.02
TAU_STAB = 1.0
SENSOR_MID = -2.0
SENSOR_WIDTH = 0.5
RATIO_FLOOR = 0.0001

F32 = jnp.float32
BF16 = jnp.bfloat16
I32 = jnp.int32
MESH = pl.DeviceIdType.MESH
NN = (((1,), (0,)), ((), ()))
NT = (((1,), (1,)), ((), ()))
VMEM_LIMIT = 60 * 1024 * 1024


def iota(shape, axis):
    return lax.broadcasted_iota(I32, shape, axis)


def split3(x):
    high = x.astype(BF16)
    rest = x - high.astype(F32)
    middle = rest.astype(BF16)
    low = (rest - middle.astype(F32)).astype(BF16)
    return high, middle, low


def split2(x):
    high = x.astype(BF16)
    return high, (x - high.astype(F32)).astype(BF16)


def dot(a, b, dims):
    return lax.dot_general(a, b, dims, preferred_element_type=F32)


def one_hot(mask):
    return jnp.where(mask, 1.0, 0.0).astype(BF16)


def element_eps(density, speed, flags):
    ids = iota((MODES, LANES), 0)
    degree = jnp.maximum(jnp.maximum(ids >> 4, (ids >> 2) & 3), ids & 3)
    squares = density * density
    totals = jnp.sum(squares, axis=0, keepdims=True) + 1e-06
    high = jnp.sum(jnp.where(degree == 3, squares, 0.0), axis=0, keepdims=True)
    sensor = jnp.log10(jnp.maximum(high / totals, RATIO_FLOOR))
    ramped = 0.5 * (1.0 + jnp.tanh((sensor - SENSOR_MID) / SENSOR_WIDTH))
    return EPS_SCALE * speed * jnp.maximum(ramped, 0.5 * flags.astype(F32))


def padded_row(row):
    source = (row * 2731) >> 16
    return source, row - source * CAP


def partner_rows(face_ref):
    pieces = [
        face_ref[end : end + 1, chunk * LANES : (chunk + 1) * LANES]
        for end in range(2)
        for chunk in range(6)
    ]
    stacked = jnp.concatenate(pieces + [jnp.zeros((LANES - 12, LANES), I32)], axis=0)
    turned = jnp.transpose(stacked.astype(F32)).astype(I32)
    high_parts = []
    low_parts = []
    for end in range(2):
        own_p, own_i = padded_row(face_ref[end : end + 1, :])
        other_p, other_i = padded_row(face_ref[1 - end : 2 - end, :])
        mine = iota((16, FACES), 0) == (own_p >> 2)
        high_parts.append(
            jnp.concatenate(
                [
                    jnp.where(mine, other_p.astype(F32), 0.0),
                    jnp.where(mine, other_i.astype(F32), 0.0),
                ],
                axis=0,
            ).astype(BF16)
        )
        columns = []
        for chunk in range(6):
            n = end * 6 + chunk
            col_p, col_i = padded_row(turned[:, n : n + 1])
            place = ((col_p & 3) << 5) + col_i
            columns.append(one_hot(iota((LANES, LANES), 1) == place))
        low_parts.append(jnp.concatenate(columns, axis=0))
    found = dot(high_parts[0], low_parts[0], NN) + dot(high_parts[1], low_parts[1], NN)
    found = found.astype(I32)
    return found[0:16], found[16:32]


def remote(src, dst, send_sem, recv_sem, where):
    return pltpu.make_async_remote_copy(
        src_ref=src,
        dst_ref=dst,
        send_sem=send_sem,
        recv_sem=recv_sem,
        device_id=where,
        device_id_type=MESH,
    )


def condense(coef_ref, coupling_ref, inner_ref, face_ref, pay):
    for j in range(EFACES):

        def body(k, sums):
            coef = coef_ref[pl.ds(k, 1), :]
            c = coupling_ref[k, j * FNODES : (j + 1) * FNODES, :].astype(F32)
            u = c * coef
            new = [sums[0] + u * c]
            for d in range(1, 8):
                new.append(sums[d] + u * pltpu.roll(c, FNODES - d, 0))
            new.append(sums[8] + u[0:8] * c[8:16])
            for comp in range(COMPS):
                new.append(sums[9 + comp] + c * (coef * inner_ref[comp, pl.ds(k, 1), :]))
            return tuple(new)

        full = jnp.zeros((FNODES, LANES), F32)
        start = (full + TAU_STAB,) + (full,) * 7 + (jnp.zeros((8, LANES), F32),) + (full,) * COMPS
        sums = lax.fori_loop(0, MODES, body, start, unroll=2)
        at = pl.ds(j * LANES, LANES)
        for d in range(9):
            pay[pl.ds(d * 16, 16 if d < 8 else 8), at] = sums[d]
        for comp in range(COMPS):
            pay[pl.ds(TRI + comp * FNODES, FNODES), at] = (
                face_ref[comp, j * FNODES : (j + 1) * FNODES, :] - sums[9 + comp]
            )
        pay[pl.ds(USED, WIDE - USED), at] = jnp.zeros((WIDE - USED, LANES), F32)


def pack_blocks(rows, z, out_ref, tail_ref, q):
    lane = iota((8, LANES), 1)
    sub = iota((8, LANES), 0)
    mine = pl.ds(z, CAP, stride=16)
    rest = rows[1, mine, :]
    x0, x1, x2 = rest[0:8], rest[8:16], rest[16:24]
    out_ref[q, 0:CAP, :] = rows[0, mine, :]
    out_ref[q, CAP : CAP + 8, :] = jnp.where(lane < 64, x0, pltpu.roll(x1, 64, 1))
    out_ref[q, CAP + 8 : CAP + 16, :] = jnp.where(
        lane < 64,
        x2,
        jnp.where(
            lane < 88, x0, jnp.where(lane < 112, pltpu.roll(x1, 24, 1), pltpu.roll(x2, 48, 1))
        ),
    )
    spread = pltpu.roll(x2, 48, 1, stride=8, stride_axis=0)
    tail_ref[q] = jnp.sum(jnp.where((lane >> 3) == sub, spread, 0.0), axis=0, keepdims=True)


def unpack_blocks(arrived_ref, tail_ref, p, rows, z):
    lane = iota((8, LANES), 1)
    sub = iota((8, LANES), 0)
    b = arrived_ref[p, CAP : CAP + 8, :]
    c = arrived_ref[p, CAP + 8 : CAP + 16, :]
    tail = jnp.broadcast_to(tail_ref[p], (8, LANES))
    spread = jnp.take_along_axis(pltpu.roll(tail, 24, 1, stride=8, stride_axis=0), 7 - sub, axis=0)
    zero = jnp.zeros((8, LANES), F32)
    base = pl.multiple_of(z * CAP, 8)
    rows[0, pl.ds(base, CAP), :] = arrived_ref[p, 0:CAP, :]
    rows[1, pl.ds(base, 8), :] = jnp.where(lane < 64, b, jnp.where(lane < 88, c, zero))
    rows[1, pl.ds(base + 8, 8), :] = jnp.where(
        lane < 64, pltpu.roll(b, 64, 1), jnp.where(lane < 88, pltpu.roll(c, 104, 1), zero)
    )
    rows[1, pl.ds(base + 16, 8), :] = jnp.where(
        lane < 64,
        c,
        jnp.where(lane < 80, pltpu.roll(c, 80, 1), jnp.where(lane < 88, spread, zero)),
    )


def pack_traces(rows, z, ret_ref, p):
    lane = iota((8, LANES), 1)
    base = pl.multiple_of(z * CAP, 8)
    y0 = rows[0, pl.ds(base, 8), :]
    y1 = rows[0, pl.ds(base + 8, 8), :]
    y2 = rows[0, pl.ds(base + 16, 8), :]
    ret_ref[p, 0:8, :] = jnp.where(lane < 64, y0, pltpu.roll(y1, 64, 1))
    ret_ref[p, 8:16, :] = jnp.where(
        lane < 64,
        y2,
        jnp.where(lane < 80, y0, jnp.where(lane < 96, pltpu.roll(y1, 16, 1), pltpu.roll(y2, 32, 1))),
    )


def unpack_traces(back_ref, q, rows, z):
    lane = iota((8, LANES), 1)
    b = back_ref[q, 0:8, :]
    c = back_ref[q, 8:16, :]
    zero = jnp.zeros((8, LANES), F32)
    y0 = jnp.where(lane < 64, b, jnp.where(lane < 80, c, zero))
    y1 = jnp.where(
        lane < 64, pltpu.roll(b, 64, 1), jnp.where(lane < 80, pltpu.roll(c, 112, 1), zero)
    )
    y2 = jnp.where(lane < 64, c, jnp.where(lane < 80, pltpu.roll(c, 96, 1), zero))
    rows[0, pl.ds(z, CAP, stride=16), :] = jnp.concatenate([y0, y1, y2], axis=0)


def block_column(grid, j):
    entries = []
    for i in range(j, FNODES):
        d, s = i - j, j
        if d > 8 or (d == 8 and s >= 8):
            d, s = FNODES - d, i
        entries.append(grid[d * 16 + s])
    return jnp.stack(entries, axis=0)


def solve_faces(grid, idle):
    scaled = []
    lower = []
    inverse = []
    for j in range(FNODES):
        column = block_column(grid, j)
        for k in range(j):
            column = column - scaled[k][j - k :] * lower[k][j - k][None]
        pivot = 1.0 / (column[0] + idle)
        inverse.append(pivot)
        scaled.append(column)
        lower.append(column * pivot[None])
    forward = []
    for i in range(FNODES):
        total = jnp.stack([grid[TRI + comp * FNODES + i] for comp in range(COMPS)], axis=0)
        for k in range(i):
            total = total - lower[k][i - k][None] * forward[k]
        forward.append(total)
    solved = [None] * FNODES
    for i in reversed(range(FNODES)):
        total = forward[i] * inverse[i][None]
        for k in range(i + 1, FNODES):
            total = total - lower[i][k - i][None] * solved[k]
        solved[i] = total
    return solved


def ring_offset(t):
    half = lax.div(t + 1, 2)
    return lax.rem(16 + half * (2 * lax.rem(t, 2) - 1), 16)


def step_kernel(
    density_ref,
    speed_ref,
    flags_ref,
    mass_ref,
    eigs_ref,
    send_ref,
    face_ref,
    coupling_hbm,
    inner_hbm,
    faceres_hbm,
    update_ref,
    traces_ref,
    coupling,
    inner,
    faceres,
    coef_ref,
    eps_out,
    eps_in,
    visc_out,
    visc_in,
    top_out,
    tops,
    slot_hot,
    row_hot,
    pay,
    pay_parts,
    rows,
    packed,
    packed_tail,
    arrived,
    arrived_tail,
    joined,
    grid,
    answer,
    returning,
    back,
    load_sem,
    send_a,
    recv_a,
    send_b,
    recv_b,
    send_c,
    recv_c,
    send_d,
    recv_d,
    send_e,
    recv_e,
    send_f,
    recv_f,
):
    me = lax.axis_index("dom")
    group = lax.axis_index("group")
    my_y = lax.div(me, N_Z)
    my_z = lax.rem(me, N_Z)
    following = {"dom": lax.rem(me + 1, N_DOM)}
    barrier = pltpu.get_barrier_semaphore()

    def greet(k, carry):
        pl.semaphore_signal(
            barrier, inc=1, device_id={"dom": lax.rem(me + k, N_DOM)}, device_id_type=MESH
        )
        return carry

    lax.fori_loop(1, N_DOM, greet, 0)

    def greet_group(k, carry):
        pl.semaphore_signal(
            barrier, inc=1, device_id={"group": lax.rem(group + k, N_GROUP)}, device_id_type=MESH
        )
        return carry

    lax.fori_loop(1, N_GROUP, greet_group, 0)
    loads = [
        pltpu.make_async_copy(coupling_hbm, coupling, load_sem.at[0]),
        pltpu.make_async_copy(inner_hbm, inner, load_sem.at[1]),
        pltpu.make_async_copy(faceres_hbm, faceres, load_sem.at[2]),
    ]
    for copy in loads:
        copy.start()

    speed = speed_ref[...]
    eps = element_eps(density_ref[...], speed, flags_ref[...])
    slots = send_ref[...]
    slots = jnp.concatenate([slots, jnp.full((N_DOM, LANES - CAP), SLOTS, I32)], axis=1)
    lane = iota((N_DOM, LANES), 1)
    values = jnp.take_along_axis(
        jnp.broadcast_to(eps, (N_DOM, LANES)), slots & (ELEM_DEV - 1), axis=1
    )
    values = jnp.where(slots < SLOTS, values, 0.0)
    values = jnp.where(lane == LANES - 1, jnp.max(speed, axis=1, keepdims=True), values)
    for q in range(N_DOM):
        eps_out[q] = values[q : q + 1, :]

    for y in range(N_Y):
        for i in range(CAP):
            column = slots[y * N_Z : (y + 1) * N_Z, i : i + 1]
            slot_hot[y, i * N_Z : (i + 1) * N_Z, :] = one_hot(iota((N_Z, SLOTS), 1) == column)

    pl.semaphore_wait(barrier, N_DOM + N_GROUP - 2)

    def send_first(k, carry):
        q = lax.rem(me + k, N_DOM)
        remote(eps_out.at[q], eps_in.at[me], send_a, recv_a, {"dom": q}).start()
        return carry

    lax.fori_loop(1, N_DOM, send_first, 0)
    eps_in[me] = eps_out[me]
    partner_p, partner_i = partner_rows(face_ref)
    others = pl.ds(0, N_DOM - 1)
    whole = remote(eps_out.at[others], eps_in.at[others], send_a, recv_a, following)
    whole.wait_recv()
    whole.wait_send()

    partner_eps = jnp.zeros((16, LANES), F32)
    top = jnp.zeros((1, LANES), F32)
    for p in range(N_DOM):
        row = eps_in[p]
        top = jnp.maximum(top, row)
        found = jnp.take_along_axis(jnp.broadcast_to(row, (16, LANES)), partner_i, axis=1)
        partner_eps = jnp.where(partner_p == p, found, partner_eps)
    for r in range(16):
        visc_out[r] = partner_eps[r : r + 1, :]
    top_out[0] = top

    def send_second(k, carry):
        p = lax.rem(me + k, N_DOM)
        remote(visc_out.at[lax.div(p, 4)], visc_in.at[me], send_b, recv_b, {"dom": p}).start()
        return carry

    lax.fori_loop(1, N_DOM, send_second, 0)

    def send_top(k, carry):
        other = lax.rem(group + k, N_GROUP)
        remote(top_out.at[0], tops.at[group], send_c, recv_c, {"group": other}).start()
        return carry

    lax.fori_loop(1, N_GROUP, send_top, 0)
    visc_in[me] = visc_out[lax.div(me, 4)]
    tops[group] = top_out[0]

    for y in range(N_Y):
        received = iota((PART, FACES), 0) + y * PART
        row_hot[y] = one_hot(
            jnp.logical_or(received == face_ref[0:1, :], received == face_ref[1:2, :])
        )
    for copy in loads:
        copy.wait()

    whole = remote(eps_in.at[others], visc_in.at[others], send_b, recv_b, following)
    whole.wait_recv()
    whole.wait_send()
    seven = pl.ds(0, N_GROUP - 1)
    whole = remote(
        tops.at[seven],
        tops.at[seven],
        send_c,
        recv_c,
        {"group": lax.rem(group + 1, N_GROUP)},
    )
    whole.wait_recv()
    whole.wait_send()

    came = jnp.concatenate([visc_in[q] for q in range(N_DOM)], axis=0)
    came = pltpu.roll(came, lax.rem(4 - lax.rem(me, 4), 4) * 32, 1)
    total = jnp.zeros((N_DOM, LANES), F32)
    for i in range(CAP):
        slot = slots[:, i : i + 1]
        here = jnp.logical_and((slot & (ELEM_DEV - 1)) == lane, slot < SLOTS)
        total = total + jnp.where(here, came[:, i : i + 1], 0.0)
    gathered = jnp.sum(total, axis=0, keepdims=True)
    nu = NU_BASE + (EFACES * eps + gathered) / (2.0 * EFACES)
    top = tops[0]
    for g in range(1, N_GROUP):
        top = jnp.maximum(top, tops[g])
    peak = jnp.max(
        jnp.where(iota((1, LANES), 1) == LANES - 1, top, 0.0), axis=1, keepdims=True
    )
    square = iota((MODES, MODES), 0) == iota((MODES, MODES), 1)
    eigs = jnp.sum(jnp.where(square, eigs_ref[...], 0.0), axis=1, keepdims=True)
    coef_ref[...] = 1.0 / (mass_ref[...] * (1.0 + speed / peak + nu * eigs))

    condense(coef_ref, coupling, inner, faceres, pay)
    for n, part in enumerate(split3(pay[...])):
        pay_parts[n] = part
    for c in range(N_Y):
        y = lax.rem(my_y + c, N_Y)
        hot = slot_hot[y]
        found = dot(hot, pay_parts[0], NT) + dot(hot, pay_parts[1], NT) + dot(hot, pay_parts[2], NT)
        rows[0] = found[:, 0:LANES]
        rows[1] = found[:, LANES:WIDE]

        def send_blocks(n, carry):
            z = lax.rem(my_z + ring_offset(N_Z - 1 - n), N_Z)
            q = y * N_Z + z
            pack_blocks(rows, z, packed, packed_tail, q)
            remote(packed.at[q], arrived.at[me], send_d, recv_d.at[c], {"dom": q}).start()
            remote(packed_tail.at[q], arrived_tail.at[me], send_e, recv_e.at[c], {"dom": q}).start()
            return carry

        lax.fori_loop(0, N_Z if c else N_Z - 1, send_blocks, 0)
        if c == 0:
            pack_blocks(rows, my_z, packed, packed_tail, me)
            arrived[me] = packed[me]
            arrived_tail[me] = packed_tail[me]

    for c in range(N_Y):
        y = lax.rem(my_y + N_Y - c, N_Y)
        sources = pl.ds(0, N_Z if c else N_Z - 1)
        remote(
            packed.at[sources], arrived.at[sources], send_d, recv_d.at[c], following
        ).wait_recv()
        remote(
            packed_tail.at[sources], arrived_tail.at[sources], send_e, recv_e.at[c], following
        ).wait_recv()

        def take_blocks(z, carry):
            unpack_blocks(arrived, arrived_tail, y * N_Z + z, rows, z)
            return carry

        lax.fori_loop(0, N_Z, take_blocks, 0, unroll=2)
        turned = jnp.concatenate(
            [jnp.transpose(rows[0]), jnp.transpose(rows[1])[0 : HEIGHT - LANES]], axis=0
        )
        stacked = jnp.concatenate(split3(turned), axis=0)
        found = dot(stacked, row_hot[y], NN)
        found = found[0:HEIGHT] + found[HEIGHT : 2 * HEIGHT] + found[2 * HEIGHT :]
        joined[...] = found if c == 0 else joined[...] + found
    remote(packed.at[others], arrived.at[others], send_d, recv_d.at[0], following).wait_send()
    remote(
        packed_tail.at[others], arrived_tail.at[others], send_e, recv_e.at[0], following
    ).wait_send()
    for chunk in range(6):
        for n in range(USED // 8):
            grid[n * 8 : n * 8 + 8, chunk, :] = joined[
                n * 8 : n * 8 + 8, chunk * LANES : (chunk + 1) * LANES
            ]
    first = face_ref[0:1, :]
    idle = jnp.concatenate(
        [first[:, chunk * LANES : (chunk + 1) * LANES] for chunk in range(6)]
        + [jnp.full((2, LANES), ROWS, I32)],
        axis=0,
    )
    idle = jnp.where(idle < ROWS, 0.0, 1.0)
    solved = solve_faces(grid, idle)
    for i in range(FNODES):
        for comp in range(COMPS):
            answer[comp * FNODES + i] = solved[i][comp]
    face_traces = jnp.concatenate([answer[:, chunk, :] for chunk in range(6)], axis=1)
    gap = jnp.zeros((LANES - COMPS * FNODES, FACES), BF16)
    high, low = split2(face_traces)
    both = jnp.concatenate([high, gap, low, gap], axis=0)

    for c in range(N_Y):
        y = lax.rem(my_y + c, N_Y)
        found = dot(row_hot[y], both, NT)
        rows[0] = found[:, 0:LANES] + found[:, LANES:WIDE]

        def send_traces(n, carry):
            z = lax.rem(my_z + ring_offset(N_Z - 1 - n), N_Z)
            p = y * N_Z + z
            pack_traces(rows, z, returning, p)
            remote(returning.at[p], back.at[me], send_f, recv_f.at[c], {"dom": p}).start()
            return carry

        lax.fori_loop(0, N_Z if c else N_Z - 1, send_traces, 0)
        if c == 0:
            pack_traces(rows, my_z, returning, me)
            back[me] = returning[me]

    for c in range(N_Y):
        y = lax.rem(my_y + N_Y - c, N_Y)
        sources = pl.ds(0, N_Z if c else N_Z - 1)
        remote(returning.at[sources], back.at[sources], send_f, recv_f.at[c], following).wait_recv()

        def take_traces(z, carry):
            unpack_traces(back, y * N_Z + z, rows, z)
            return carry

        lax.fori_loop(0, N_Z, take_traces, 0, unroll=2)
        turned = jnp.transpose(rows[0])[0 : COMPS * FNODES]
        stacked = jnp.concatenate(split2(turned), axis=0)
        found = dot(stacked, slot_hot[y], NN)
        found = found[0 : COMPS * FNODES] + found[COMPS * FNODES :]
        for comp in range(COMPS):
            for j in range(EFACES):
                piece = found[
                    comp * FNODES : (comp + 1) * FNODES, j * LANES : (j + 1) * LANES
                ]
                at = slice(j * FNODES, (j + 1) * FNODES)
                traces_ref[comp, at, :] = piece if c == 0 else traces_ref[comp, at, :] + piece
    remote(returning.at[others], back.at[others], send_f, recv_f.at[0], following).wait_send()

    def substitute(k, carry):
        c = coupling[k].astype(F32)
        coef = coef_ref[pl.ds(k, 1), :]
        for comp in range(COMPS):
            pulled = jnp.sum(c * traces_ref[comp], axis=0, keepdims=True)
            update_ref[comp, pl.ds(k, 1), :] = coef * (inner[comp, pl.ds(k, 1), :] - pulled)
        return carry

    lax.fori_loop(0, MODES, substitute, 0, unroll=2)


def local(
    density_modes,
    wave_speed,
    shock_flags,
    elem_mass,
    stiff_eigs,
    coupling,
    interior_res,
    face_res,
    send_rows,
    face_rows,
):
    vmem = pl.BlockSpec(memory_space=pltpu.VMEM)
    anywhere = pl.BlockSpec(memory_space=pl.ANY)
    dma = pltpu.SemaphoreType.DMA
    return pl.pallas_call(
        step_kernel,
        out_shape=(
            jax.ShapeDtypeStruct((COMPS, MODES, LANES), F32),
            jax.ShapeDtypeStruct((COMPS, TRACE, LANES), F32),
        ),
        in_specs=[vmem] * 7 + [anywhere] * 3,
        out_specs=(vmem, vmem),
        scratch_shapes=[
            pltpu.VMEM((MODES, TRACE, LANES), BF16),
            pltpu.VMEM((COMPS, MODES, LANES), F32),
            pltpu.VMEM((COMPS, TRACE, LANES), F32),
            pltpu.VMEM((MODES, LANES), F32),
            pltpu.VMEM((N_DOM, 1, LANES), F32),
            pltpu.VMEM((N_DOM, 1, LANES), F32),
            pltpu.VMEM((16, 1, LANES), F32),
            pltpu.VMEM((N_DOM, 1, LANES), F32),
            pltpu.VMEM((1, 1, LANES), F32),
            pltpu.VMEM((N_GROUP, 1, LANES), F32),
            pltpu.VMEM((N_Y, PART, SLOTS), BF16),
            pltpu.VMEM((N_Y, PART, FACES), BF16),
            pltpu.VMEM((WIDE, SLOTS), F32),
            pltpu.VMEM((3, WIDE, SLOTS), BF16),
            pltpu.VMEM((2, PART, LANES), F32),
            pltpu.VMEM((N_DOM, OUT_TILE, LANES), F32),
            pltpu.VMEM((N_DOM, 1, LANES), F32),
            pltpu.VMEM((N_DOM, OUT_TILE, LANES), F32),
            pltpu.VMEM((N_DOM, 1, LANES), F32),
            pltpu.VMEM((HEIGHT, FACES), F32),
            pltpu.VMEM((USED, 8, LANES), F32),
            pltpu.VMEM((COMPS * FNODES, 8, LANES), F32),
            pltpu.VMEM((N_DOM, RET_TILE, LANES), F32),
            pltpu.VMEM((N_DOM, RET_TILE, LANES), F32),
            dma((3,)),
            dma,
            dma,
            dma,
            dma,
            dma,
            dma,
            dma,
            dma((N_Y,)),
            dma,
            dma((N_Y,)),
            dma,
            dma((N_Y,)),
        ],
        compiler_params=pltpu.CompilerParams(
            collective_id=0, has_side_effects=True, vmem_limit_bytes=VMEM_LIMIT
        ),
        name="newton_step",
    )(
        density_modes,
        wave_speed[None, :],
        shock_flags[None, :],
        elem_mass[None, :],
        stiff_eigs[None, :],
        send_rows.reshape(N_DOM, CAP),
        face_rows,
        coupling,
        interior_res,
        face_res,
    )


def solution(mesh):
    return jax.shard_map(
        local,
        mesh=mesh,
        in_specs=(
            P(None, ("group", "dom")),
            P(("group", "dom")),
            P(("group", "dom")),
            P(("group", "dom")),
            P(),
            P(None, None, ("group", "dom")),
            P(None, None, ("group", "dom")),
            P(None, None, ("group", "dom")),
            P(("group", "dom")),
            P(None, ("group", "dom")),
        ),
        out_specs=(P(None, None, ("group", "dom")), P(None, None, ("group", "dom"))),
        check_vma=False,
    )
```

```python
import jax
import jax.numpy as jnp
from jax import lax
from jax.experimental import pallas as pl
from jax.experimental.pallas import tpu as pltpu
from jax.sharding import PartitionSpec as P

MODES = 64
FNODES = 16
COMPS = 5
EFACES = 6
TRACE = 96
ELEM_DEV = 128
SLOTS = EFACES * ELEM_DEV
CAP = 24
N_DOM = 64
N_GROUP = 8
ROWS = N_DOM * CAP
FACES = 768
TRI = 136
USED = 216
N_Z = 16
N_Y = N_DOM // N_Z
PART = N_Z * CAP
LANES = 128
HALF = 96
REST_TILE = 17
RET_TILE = 15

EPS_SCALE = 0.1
NU_BASE = 0.02
TAU_STAB = 1.0
SENSOR_MID = -2.0
SENSOR_WIDTH = 0.5
RATIO_FLOOR = 0.0001

F32 = jnp.float32
BF16 = jnp.bfloat16
I32 = jnp.int32
MESH = pl.DeviceIdType.MESH
NN = (((1,), (0,)), ((), ()))
NT = (((1,), (1,)), ((), ()))
VMEM_LIMIT = 60 * 1024 * 1024


def iota(shape, axis):
    return lax.broadcasted_iota(I32, shape, axis)


def split3(x):
    high = x.astype(BF16)
    rest = x - high.astype(F32)
    middle = rest.astype(BF16)
    low = (rest - middle.astype(F32)).astype(BF16)
    return high, middle, low


def split2(x):
    high = x.astype(BF16)
    return high, (x - high.astype(F32)).astype(BF16)


def dot(a, b, dims):
    return lax.dot_general(a, b, dims, preferred_element_type=F32)


def one_hot(mask):
    return jnp.where(mask, 1.0, 0.0).astype(BF16)


def element_eps(density, speed, flags):
    ids = iota((MODES, LANES), 0)
    degree = jnp.maximum(jnp.maximum(ids >> 4, (ids >> 2) & 3), ids & 3)
    squares = density * density
    totals = jnp.sum(squares, axis=0, keepdims=True) + 1e-06
    high = jnp.sum(jnp.where(degree == 3, squares, 0.0), axis=0, keepdims=True)
    sensor = jnp.log10(jnp.maximum(high / totals, RATIO_FLOOR))
    ramped = 0.5 * (1.0 + jnp.tanh((sensor - SENSOR_MID) / SENSOR_WIDTH))
    return EPS_SCALE * speed * jnp.maximum(ramped, 0.5 * flags.astype(F32))


def padded_row(row):
    source = (row * 2731) >> 16
    return source, row - source * CAP


def partner_rows(face_ref):
    pieces = [
        face_ref[end : end + 1, chunk * LANES : (chunk + 1) * LANES]
        for end in range(2)
        for chunk in range(6)
    ]
    stacked = jnp.concatenate(pieces + [jnp.zeros((LANES - 12, LANES), I32)], axis=0)
    turned = jnp.transpose(stacked.astype(F32)).astype(I32)
    high_parts = []
    low_parts = []
    for end in range(2):
        own_p, own_i = padded_row(face_ref[end : end + 1, :])
        other_p, other_i = padded_row(face_ref[1 - end : 2 - end, :])
        mine = iota((16, FACES), 0) == (own_p >> 2)
        high_parts.append(
            jnp.concatenate(
                [
                    jnp.where(mine, other_p.astype(F32), 0.0),
                    jnp.where(mine, other_i.astype(F32), 0.0),
                ],
                axis=0,
            ).astype(BF16)
        )
        columns = []
        for chunk in range(6):
            n = end * 6 + chunk
            col_p, col_i = padded_row(turned[:, n : n + 1])
            place = ((col_p & 3) << 5) + col_i
            columns.append(one_hot(iota((LANES, LANES), 1) == place))
        low_parts.append(jnp.concatenate(columns, axis=0))
    found = dot(high_parts[0], low_parts[0], NN) + dot(high_parts[1], low_parts[1], NN)
    found = found.astype(I32)
    return found[0:16], found[16:32]


def remote(src, dst, send_sem, recv_sem, where):
    return pltpu.make_async_remote_copy(
        src_ref=src,
        dst_ref=dst,
        send_sem=send_sem,
        recv_sem=recv_sem,
        device_id=where,
        device_id_type=MESH,
    )


def block_row(i, j):
    d = (i - j) % 8
    if i >= 8 > j:
        return 64 + d * 8 + j
    base = 32 if j >= 8 else 0
    low, high = j % 8, i % 8
    if d < 4:
        return base + d * 8 + low
    if d > 4:
        return base + (8 - d) * 8 + high
    return 128 + (high if base else low)


def condense_blocks(coef_ref, coupling_ref, pay_a, pay_b):
    sub = iota((8, LANES), 0)
    for j in range(EFACES):

        def body(k, sums):
            coef = coef_ref[pl.ds(k, 1), :]
            c = coupling_ref[k, j * FNODES : (j + 1) * FNODES, :].astype(F32)
            c0, c1 = c[0:8], c[8:16]
            u0, u1 = c0 * coef, c1 * coef
            new = []
            for d in range(5):
                new.append(sums[len(new)] + u0 * (pltpu.roll(c0, 8 - d, 0) if d else c0))
            for d in range(5):
                new.append(sums[len(new)] + u1 * (pltpu.roll(c1, 8 - d, 0) if d else c1))
            for d in range(8):
                new.append(sums[len(new)] + u0 * (pltpu.roll(c1, 8 - d, 0) if d else c1))
            return tuple(new)

        zero = jnp.zeros((8, LANES), F32)
        start = [zero] * 18
        start[0] = start[5] = zero + TAU_STAB
        sums = lax.fori_loop(0, MODES, body, tuple(start), unroll=8)
        at = pl.ds(j * LANES, LANES)
        for d in range(4):
            pay_a[pl.ds(d * 8, 8), at] = sums[d]
            pay_a[pl.ds(32 + d * 8, 8), at] = sums[5 + d]
        for d in range(8):
            pay_a[pl.ds(64 + d * 8, 8), at] = sums[10 + d]
        pay_b[pl.ds(0, 8), at] = jnp.where(sub < 4, sums[4], sums[9])


def condense_loads(weighted_ref, coupling_ref, face_ref, pay_b):
    for j in range(EFACES):

        def body(k, sums):
            c = coupling_ref[k, j * FNODES : (j + 1) * FNODES, :].astype(F32)
            return tuple(
                sums[comp] + c * weighted_ref[comp, pl.ds(k, 1), :] for comp in range(COMPS)
            )

        start = (jnp.zeros((FNODES, LANES), F32),) * COMPS
        sums = lax.fori_loop(0, MODES, body, start, unroll=8)
        at = pl.ds(j * LANES, LANES)
        for comp in range(COMPS):
            pay_b[pl.ds(8 + comp * FNODES, FNODES), at] = (
                face_ref[comp, j * FNODES : (j + 1) * FNODES, :] - sums[comp]
            )
        pay_b[pl.ds(88, LANES - 88), at] = jnp.zeros((LANES - 88, LANES), F32)


def pick(hot, parts):
    found = dot(hot, parts, NT)
    return found[:, 0:LANES] + found[:, LANES : 2 * LANES] + found[:, 2 * LANES :]


def pack_rest(rows, z, out_ref, q):
    lane = iota((8, LANES), 1)
    sub = iota((8, LANES), 0)
    rest = rows[pl.ds(z, CAP, stride=16), :]
    x0, x1, x2 = rest[0:8], rest[8:16], rest[16:24]
    out_ref[q, 0:8, :] = jnp.where(lane < 64, x0, pltpu.roll(x1, 64, 1))
    out_ref[q, 8:16, :] = jnp.where(
        lane < 64,
        x2,
        jnp.where(
            lane < 88, x0, jnp.where(lane < 112, pltpu.roll(x1, 24, 1), pltpu.roll(x2, 48, 1))
        ),
    )
    spread = pltpu.roll(x2, 48, 1, stride=8, stride_axis=0)
    out_ref[q, 16:17, :] = jnp.sum(
        jnp.where((lane >> 3) == sub, spread, 0.0), axis=0, keepdims=True
    )


def unpack_rest(arrived_ref, p, rows, z):
    lane = iota((8, LANES), 1)
    sub = iota((8, LANES), 0)
    b = arrived_ref[p, 0:8, :]
    c = arrived_ref[p, 8:16, :]
    tail = jnp.broadcast_to(arrived_ref[p, 16:17, :], (8, LANES))
    spread = jnp.take_along_axis(pltpu.roll(tail, 24, 1, stride=8, stride_axis=0), 7 - sub, axis=0)
    zero = jnp.zeros((8, LANES), F32)
    base = pl.multiple_of(z * CAP, 8)
    rows[pl.ds(base, 8), :] = jnp.where(lane < 64, b, jnp.where(lane < 88, c, zero))
    rows[pl.ds(base + 8, 8), :] = jnp.where(
        lane < 64, pltpu.roll(b, 64, 1), jnp.where(lane < 88, pltpu.roll(c, 104, 1), zero)
    )
    rows[pl.ds(base + 16, 8), :] = jnp.where(
        lane < 64,
        c,
        jnp.where(lane < 80, pltpu.roll(c, 80, 1), jnp.where(lane < 88, spread, zero)),
    )


def pack_traces(rows, z, ret_ref, p):
    lane = iota((8, LANES), 1)
    base = pl.multiple_of(z * CAP, 8)
    y0 = rows[pl.ds(base, 8), :]
    y1 = rows[pl.ds(base + 8, 8), :]
    y2 = rows[pl.ds(base + 16, 8), :]
    ret_ref[p, 0:8, :] = jnp.where(lane < 64, y0, pltpu.roll(y1, 64, 1))
    second = jnp.where(
        lane < 64,
        y2,
        jnp.where(lane < 80, y0, jnp.where(lane < 96, pltpu.roll(y1, 16, 1), pltpu.roll(y2, 32, 1))),
    )
    last = jnp.broadcast_to(pltpu.roll(second, 16, 1)[7:8], (8, LANES))
    last = pltpu.roll(last, 0, 1, stride=16, stride_axis=0)
    ret_ref[p, 8:15, :] = jnp.where(lane < 112, second, last)[0:7]


def unpack_traces(back_ref, q, rows, z):
    lane = iota((8, LANES), 1)
    sub = iota((8, LANES), 0)
    zero = jnp.zeros((8, LANES), F32)
    b = back_ref[q, 0:8, :]
    c = jnp.concatenate([back_ref[q, 8:15, :], zero[0:1]], axis=0)
    last = pltpu.roll(jnp.take_along_axis(c, 7 - sub, axis=0), 0, 1, stride=16, stride_axis=0)
    last = jnp.sum(jnp.where((lane >> 4) == sub - 1, last, 0.0), axis=0, keepdims=True)
    c = jnp.where(sub < 7, c, jnp.broadcast_to(last, (8, LANES)))
    y0 = jnp.where(lane < 64, b, jnp.where(lane < 80, c, zero))
    y1 = jnp.where(
        lane < 64, pltpu.roll(b, 64, 1), jnp.where(lane < 80, pltpu.roll(c, 112, 1), zero)
    )
    y2 = jnp.where(lane < 64, c, jnp.where(lane < 80, pltpu.roll(c, 96, 1), zero))
    rows[pl.ds(z, CAP, stride=16), :] = jnp.concatenate([y0, y1, y2], axis=0)


def solve_faces(grid, idle):
    scaled = []
    lower = []
    inverse = []
    for j in range(FNODES):
        column = jnp.stack([grid[block_row(i, j)] for i in range(j, FNODES)], axis=0)
        for k in range(j):
            column = column - scaled[k][j - k :] * lower[k][j - k][None]
        pivot = 1.0 / (column[0] + idle)
        inverse.append(pivot)
        scaled.append(column)
        lower.append(column * pivot[None])
    forward = []
    for i in range(FNODES):
        total = jnp.stack([grid[TRI + comp * FNODES + i] for comp in range(COMPS)], axis=0)
        for k in range(i):
            total = total - lower[k][i - k][None] * forward[k]
        forward.append(total)
    solved = [None] * FNODES
    for i in reversed(range(FNODES)):
        total = forward[i] * inverse[i][None]
        for k in range(i + 1, FNODES):
            total = total - lower[i][k - i][None] * solved[k]
        solved[i] = total
    return solved


def ring_offset(n):
    t = N_Z - 1 - n
    half = lax.div(t + 1, 2)
    return lax.rem(16 + half * (2 * lax.rem(t, 2) - 1), 16)


def spread_slots(lists, slots):
    lane = iota((4, LANES), 1)
    rows = [lists[pl.ds(a, 4, stride=3), :] for a in range(3)]
    for z in range(N_Z):
        a, b = divmod(z * CAP, LANES)
        value = pltpu.roll(rows[a], LANES - b, 1) if b else rows[a]
        if b + CAP > LANES:
            value = jnp.where(lane < LANES - b, value, pltpu.roll(rows[a + 1], LANES - b, 1))
        slots[pl.ds(z, 4, stride=N_Z), :] = jnp.where(lane < CAP, value, SLOTS)


def step_kernel(
    density_hbm,
    speed_hbm,
    flags_hbm,
    mass_hbm,
    eigs_hbm,
    send_hbm,
    face_hbm,
    coupling_hbm,
    inner_hbm,
    faceres_hbm,
    traces_ref,
    coef_ref,
    density,
    speed_ref,
    flags,
    mass,
    eigs_ref,
    lists,
    face_ref,
    coupling,
    inner,
    faceres,
    slots_ref,
    weighted,
    eps_out,
    eps_in,
    visc_out,
    visc_in,
    top_out,
    tops,
    slot_hot,
    row_hot,
    pay_a,
    pay_b,
    parts_a,
    parts_b,
    rows,
    whole_out,
    whole_in,
    rest_out,
    rest_in,
    joined_a,
    joined_b,
    grid,
    answer,
    returning,
    back,
    load_sem,
    send_a,
    recv_a,
    send_b,
    recv_b,
    send_c,
    recv_c,
    send_d,
    recv_d,
    send_e,
    recv_e,
    send_f,
    recv_f,
):
    me = lax.axis_index("dom")
    group = lax.axis_index("group")
    my_y = lax.div(me, N_Z)
    my_z = lax.rem(me, N_Z)
    following = {"dom": lax.rem(me + 1, N_DOM)}
    barrier = pltpu.get_barrier_semaphore()

    def each_peer(act):
        def one_z(n, carry):
            z = lax.rem(my_z + ring_offset(n), N_Z)
            for dy in (2, 1, 3, 0):
                act(lax.rem(my_y + dy, N_Y) * N_Z + z)
            return carry

        lax.fori_loop(0, N_Z - 1, one_z, 0)
        for dy in (2, 1, 3):
            act(lax.rem(my_y + dy, N_Y) * N_Z + my_z)

    def each_group(act):
        def one(k, carry):
            act(lax.rem(group + k, N_GROUP))
            return carry

        lax.fori_loop(1, N_GROUP, one, 0)

    each_peer(
        lambda q: pl.semaphore_signal(barrier, inc=1, device_id={"dom": q}, device_id_type=MESH)
    )
    each_group(
        lambda g: pl.semaphore_signal(barrier, inc=1, device_id={"group": g}, device_id_type=MESH)
    )
    loads = [
        pltpu.make_async_copy(source, target, load_sem.at[n])
        for n, (source, target) in enumerate(
            (
                (density_hbm, density),
                (speed_hbm, speed_ref),
                (flags_hbm, flags),
                (send_hbm, lists),
                (face_hbm, face_ref),
                (mass_hbm, mass),
                (eigs_hbm, eigs_ref),
                (coupling_hbm, coupling),
                (inner_hbm, inner),
                (faceres_hbm, faceres),
            )
        )
    ]
    for copy in loads:
        copy.start()
    for copy in loads[:5]:
        copy.wait()

    speed = speed_ref[...]
    eps = element_eps(density[...], speed, flags[...])
    spread_slots(lists, slots_ref)
    slots = slots_ref[...]
    lane = iota((N_DOM, LANES), 1)
    values = jnp.take_along_axis(
        jnp.broadcast_to(eps, (N_DOM, LANES)), slots & (ELEM_DEV - 1), axis=1
    )
    values = jnp.where(slots < SLOTS, values, 0.0)
    values = jnp.where(lane == LANES - 1, jnp.max(speed, axis=1, keepdims=True), values)
    for q in range(N_DOM):
        eps_out[q] = values[q : q + 1, :]

    for y in range(N_Y):
        for i in range(CAP):
            column = slots[y * N_Z : (y + 1) * N_Z, i : i + 1]
            slot_hot[y, i * N_Z : (i + 1) * N_Z, :] = one_hot(iota((N_Z, SLOTS), 1) == column)

    pl.semaphore_wait(barrier, N_DOM + N_GROUP - 2)
    each_peer(
        lambda q: remote(eps_out.at[q], eps_in.at[me], send_a, recv_a, {"dom": q}).start()
    )
    eps_in[me] = eps_out[me]
    partner_p, partner_i = partner_rows(face_ref)
    others = pl.ds(0, N_DOM - 1)
    whole = remote(eps_out.at[others], eps_in.at[others], send_a, recv_a, following)
    whole.wait_recv()
    whole.wait_send()

    partner_eps = jnp.zeros((16, LANES), F32)
    top = jnp.zeros((1, LANES), F32)
    for p in range(N_DOM):
        row = eps_in[p]
        top = jnp.maximum(top, row)
        found = jnp.take_along_axis(jnp.broadcast_to(row, (16, LANES)), partner_i, axis=1)
        partner_eps = jnp.where(partner_p == p, found, partner_eps)
    for r in range(16):
        visc_out[r] = partner_eps[r : r + 1, :]
    top_out[0] = top
    each_peer(
        lambda p: remote(
            visc_out.at[lax.div(p, 4)], visc_in.at[me], send_b, recv_b, {"dom": p}
        ).start()
    )
    each_group(
        lambda g: remote(top_out.at[0], tops.at[group], send_c, recv_c, {"group": g}).start()
    )
    visc_in[me] = visc_out[lax.div(me, 4)]
    tops[group] = top_out[0]

    for y in range(N_Y):
        received = iota((PART, FACES), 0) + y * PART
        row_hot[y] = one_hot(
            jnp.logical_or(received == face_ref[0:1, :], received == face_ref[1:2, :])
        )
    for copy in loads[5:]:
        copy.wait()

    whole = remote(eps_in.at[others], visc_in.at[others], send_b, recv_b, following)
    whole.wait_recv()
    whole.wait_send()
    seven = pl.ds(0, N_GROUP - 1)
    whole = remote(
        tops.at[seven],
        tops.at[seven],
        send_c,
        recv_c,
        {"group": lax.rem(group + 1, N_GROUP)},
    )
    whole.wait_recv()
    whole.wait_send()

    came = jnp.concatenate([visc_in[q] for q in range(N_DOM)], axis=0)
    came = pltpu.roll(came, lax.rem(4 - lax.rem(me, 4), 4) * 32, 1)
    total = jnp.zeros((N_DOM, LANES), F32)
    for i in range(CAP):
        slot = slots[:, i : i + 1]
        here = jnp.logical_and((slot & (ELEM_DEV - 1)) == lane, slot < SLOTS)
        total = total + jnp.where(here, came[:, i : i + 1], 0.0)
    gathered = jnp.sum(total, axis=0, keepdims=True)
    nu = NU_BASE + (EFACES * eps + gathered) / (2.0 * EFACES)
    top = tops[0]
    for g in range(1, N_GROUP):
        top = jnp.maximum(top, tops[g])
    peak = jnp.max(jnp.where(iota((1, LANES), 1) == LANES - 1, top, 0.0), axis=1, keepdims=True)
    square = iota((MODES, MODES), 0) == iota((MODES, MODES), 1)
    eigs = jnp.sum(jnp.where(square, eigs_ref[...], 0.0), axis=1, keepdims=True)
    coef = 1.0 / (mass[...] * (1.0 + speed / peak + nu * eigs))
    coef_ref[...] = coef

    condense_blocks(coef_ref, coupling, pay_a, pay_b)
    parts_a[...] = jnp.concatenate(split3(pay_a[...]), axis=0)
    for c in range(N_Y):
        y = lax.rem(my_y + c, N_Y)
        rows[...] = pick(slot_hot[y], parts_a[...])

        def send_whole(n, carry):
            z = lax.rem(my_z + ring_offset(n), N_Z)
            q = y * N_Z + z
            whole_out[q] = rows[pl.ds(z, CAP, stride=16), :]
            remote(whole_out.at[q], whole_in.at[me], send_d, recv_d.at[c], {"dom": q}).start()
            return carry

        lax.fori_loop(0, N_Z if c else N_Z - 1, send_whole, 0)
        if c == 0:
            whole_in[me] = rows[pl.ds(my_z, CAP, stride=16), :]
    weighted[...] = inner[...] * coef[None]
    condense_loads(weighted, coupling, faceres, pay_b)
    parts_b[...] = jnp.concatenate(split3(pay_b[...]), axis=0)
    for c in range(N_Y):
        y = lax.rem(my_y + c, N_Y)
        rows[...] = pick(slot_hot[y], parts_b[...])

        def send_rest(n, carry):
            z = lax.rem(my_z + ring_offset(n), N_Z)
            q = y * N_Z + z
            pack_rest(rows, z, rest_out, q)
            remote(rest_out.at[q], rest_in.at[me], send_e, recv_e.at[c], {"dom": q}).start()
            return carry

        lax.fori_loop(0, N_Z if c else N_Z - 1, send_rest, 0)
        if c == 0:
            pack_rest(rows, my_z, rest_in, me)

    def to_grid(joined, start, height):
        for chunk in range(6):
            for n in range(height // 8):
                grid[start + n * 8 : start + n * 8 + 8, chunk, :] = joined[
                    n * 8 : n * 8 + 8, chunk * LANES : (chunk + 1) * LANES
                ]

    for c in range(N_Y):
        y = lax.rem(my_y + N_Y - c, N_Y)
        sources = pl.ds(0, N_Z if c else N_Z - 1)
        remote(
            whole_out.at[sources], whole_in.at[sources], send_d, recv_d.at[c], following
        ).wait_recv()
        came = whole_in[pl.ds(pl.multiple_of(y * N_Z, N_Z), N_Z)].reshape(PART, LANES)
        stacked = jnp.concatenate(split3(jnp.transpose(came)), axis=0)
        found = dot(stacked, row_hot[y], NN)
        found = found[0:LANES] + found[LANES : 2 * LANES] + found[2 * LANES :]
        joined_a[...] = found if c == 0 else joined_a[...] + found
    to_grid(joined_a, 0, LANES)
    remote(whole_out.at[others], whole_in.at[others], send_d, recv_d.at[0], following).wait_send()
    for c in range(N_Y):
        y = lax.rem(my_y + N_Y - c, N_Y)
        sources = pl.ds(0, N_Z if c else N_Z - 1)
        remote(
            rest_out.at[sources], rest_in.at[sources], send_e, recv_e.at[c], following
        ).wait_recv()

        def take_rest(z, carry):
            unpack_rest(rest_in, y * N_Z + z, rows, z)
            return carry

        lax.fori_loop(0, N_Z, take_rest, 0, unroll=2)
        stacked = jnp.concatenate(split3(jnp.transpose(rows[...])[0:HALF]), axis=0)
        found = dot(stacked, row_hot[y], NN)
        found = found[0:HALF] + found[HALF : 2 * HALF] + found[2 * HALF :]
        joined_b[...] = found if c == 0 else joined_b[...] + found
    to_grid(joined_b, LANES, USED - LANES)
    first = face_ref[0:1, :]
    idle = jnp.concatenate(
        [first[:, chunk * LANES : (chunk + 1) * LANES] for chunk in range(6)]
        + [jnp.full((2, LANES), ROWS, I32)],
        axis=0,
    )
    idle = jnp.where(idle < ROWS, 0.0, 1.0)
    solved = solve_faces(grid, idle)
    for i in range(FNODES):
        for comp in range(COMPS):
            answer[comp * FNODES + i] = solved[i][comp]
    face_traces = jnp.concatenate([answer[:, chunk, :] for chunk in range(6)], axis=1)
    gap = jnp.zeros((LANES - COMPS * FNODES, FACES), BF16)
    high, low = split2(face_traces)
    both = jnp.concatenate([high, gap, low, gap], axis=0)

    for c in range(N_Y):
        y = lax.rem(my_y + c, N_Y)
        found = dot(row_hot[y], both, NT)
        rows[...] = found[:, 0:LANES] + found[:, LANES : 2 * LANES]

        def send_traces(n, carry):
            z = lax.rem(my_z + ring_offset(n), N_Z)
            p = y * N_Z + z
            pack_traces(rows, z, returning, p)
            remote(returning.at[p], back.at[me], send_f, recv_f.at[c], {"dom": p}).start()
            return carry

        lax.fori_loop(0, N_Z if c else N_Z - 1, send_traces, 0)
        if c == 0:
            pack_traces(rows, my_z, back, me)

    for c in range(N_Y):
        y = lax.rem(my_y + N_Y - c, N_Y)
        sources = pl.ds(0, N_Z if c else N_Z - 1)
        remote(returning.at[sources], back.at[sources], send_f, recv_f.at[c], following).wait_recv()

        def take_traces(z, carry):
            unpack_traces(back, y * N_Z + z, rows, z)
            return carry

        lax.fori_loop(0, N_Z, take_traces, 0, unroll=2)
        turned = jnp.transpose(rows[...])[0 : COMPS * FNODES]
        stacked = jnp.concatenate(split2(turned), axis=0)
        found = dot(stacked, slot_hot[y], NN)
        found = found[0 : COMPS * FNODES] + found[COMPS * FNODES :]
        for comp in range(COMPS):
            for j in range(EFACES):
                piece = found[comp * FNODES : (comp + 1) * FNODES, j * LANES : (j + 1) * LANES]
                at = slice(j * FNODES, (j + 1) * FNODES)
                traces_ref[comp, at, :] = piece if c == 0 else traces_ref[comp, at, :] + piece
    remote(rest_out.at[others], rest_in.at[others], send_e, recv_e.at[0], following).wait_send()
    remote(returning.at[others], back.at[others], send_f, recv_f.at[0], following).wait_send()


def update_kernel(traces_in, coef_ref, coupling_ref, inner_ref, update_ref, traces_ref):
    traces_ref[...] = traces_in[...]

    def substitute(k, carry):
        c = coupling_ref[k].astype(F32)
        coef = coef_ref[pl.ds(k, 1), :]
        for comp in range(COMPS):
            pulled = jnp.sum(c * traces_in[comp], axis=0, keepdims=True)
            update_ref[comp, pl.ds(k, 1), :] = coef * (inner_ref[comp, pl.ds(k, 1), :] - pulled)
        return carry

    lax.fori_loop(0, MODES, substitute, 0, unroll=4)


def local(
    density_modes,
    wave_speed,
    shock_flags,
    elem_mass,
    stiff_eigs,
    coupling,
    interior_res,
    face_res,
    send_rows,
    face_rows,
):
    vmem = pl.BlockSpec(memory_space=pltpu.VMEM)
    anywhere = pl.BlockSpec(memory_space=pltpu.HBM)
    dma = pltpu.SemaphoreType.DMA
    traces, coef = pl.pallas_call(
        step_kernel,
        out_shape=(
            jax.ShapeDtypeStruct((COMPS, TRACE, LANES), F32),
            jax.ShapeDtypeStruct((MODES, LANES), F32),
        ),
        in_specs=[anywhere] * 10,
        out_specs=(vmem, vmem),
        scratch_shapes=[
            pltpu.VMEM((MODES, LANES), F32),
            pltpu.VMEM((1, LANES), F32),
            pltpu.VMEM((1, LANES), I32),
            pltpu.VMEM((1, LANES), F32),
            pltpu.VMEM((1, MODES), F32),
            pltpu.VMEM((12, LANES), I32),
            pltpu.VMEM((2, FACES), I32),
            pltpu.VMEM((MODES, TRACE, LANES), BF16),
            pltpu.VMEM((COMPS, MODES, LANES), F32),
            pltpu.VMEM((COMPS, TRACE, LANES), F32),
            pltpu.VMEM((N_DOM, LANES), I32),
            pltpu.VMEM((COMPS, MODES, LANES), F32),
            pltpu.VMEM((N_DOM, 1, LANES), F32),
            pltpu.VMEM((N_DOM, 1, LANES), F32),
            pltpu.VMEM((16, 1, LANES), F32),
            pltpu.VMEM((N_DOM, 1, LANES), F32),
            pltpu.VMEM((1, 1, LANES), F32),
            pltpu.VMEM((N_GROUP, 1, LANES), F32),
            pltpu.VMEM((N_Y, PART, SLOTS), BF16),
            pltpu.VMEM((N_Y, PART, FACES), BF16),
            pltpu.VMEM((LANES, SLOTS), F32),
            pltpu.VMEM((LANES, SLOTS), F32),
            pltpu.VMEM((3 * LANES, SLOTS), BF16),
            pltpu.VMEM((3 * LANES, SLOTS), BF16),
            pltpu.VMEM((PART, LANES), F32),
            pltpu.VMEM((N_DOM, CAP, LANES), F32),
            pltpu.VMEM((N_DOM, CAP, LANES), F32),
            pltpu.VMEM((N_DOM, REST_TILE, LANES), F32),
            pltpu.VMEM((N_DOM, REST_TILE, LANES), F32),
            pltpu.VMEM((LANES, FACES), F32),
            pltpu.VMEM((HALF, FACES), F32),
            pltpu.VMEM((USED, 8, LANES), F32),
            pltpu.VMEM((COMPS * FNODES, 8, LANES), F32),
            pltpu.VMEM((N_DOM, RET_TILE, LANES), F32),
            pltpu.VMEM((N_DOM, RET_TILE, LANES), F32),
            dma((10,)),
            dma,
            dma,
            dma,
            dma,
            dma,
            dma,
            dma,
            dma((N_Y,)),
            dma,
            dma((N_Y,)),
            dma,
            dma((N_Y,)),
        ],
        compiler_params=pltpu.CompilerParams(
            collective_id=0, has_side_effects=True, vmem_limit_bytes=VMEM_LIMIT
        ),
        name="newton_step",
    )(
        density_modes,
        wave_speed[None, :],
        shock_flags[None, :],
        elem_mass[None, :],
        stiff_eigs[None, :],
        send_rows.reshape(12, LANES),
        face_rows,
        coupling,
        interior_res,
        face_res,
    )
    return pl.pallas_call(
        update_kernel,
        out_shape=(
            jax.ShapeDtypeStruct((COMPS, MODES, LANES), F32),
            jax.ShapeDtypeStruct((COMPS, TRACE, LANES), F32),
        ),
        in_specs=[vmem] * 4,
        out_specs=(vmem, vmem),
        compiler_params=pltpu.CompilerParams(vmem_limit_bytes=16 * 1024 * 1024),
        name="back_substitute",
    )(traces, coef, coupling, interior_res)


def solution(mesh):
    return jax.shard_map(
        local,
        mesh=mesh,
        in_specs=(
            P(None, ("group", "dom")),
            P(("group", "dom")),
            P(("group", "dom")),
            P(("group", "dom")),
            P(),
            P(None, None, ("group", "dom")),
            P(None, None, ("group", "dom")),
            P(None, None, ("group", "dom")),
            P(("group", "dom")),
            P(None, ("group", "dom")),
        ),
        out_specs=(P(None, None, ("group", "dom")), P(None, None, ("group", "dom"))),
        check_vma=False,
    )
```

```python
import jax
import jax.numpy as jnp
from jax import lax
from jax.experimental import pallas as pl
from jax.experimental.pallas import tpu as pltpu
from jax.sharding import PartitionSpec as P

MODES = 64
FNODES = 16
COMPS = 5
EFACES = 6
TRACE = 96
ELEM_DEV = 128
SLOTS = EFACES * ELEM_DEV
CAP = 24
N_DOM = 64
N_GROUP = 8
ROWS = N_DOM * CAP
FACES = 768
TRI = 136
USED = 216
N_Z = 16
N_Y = N_DOM // N_Z
PART = N_Z * CAP
LANES = 128
HALF = 48
EARLY = 2
FIRST_TILE = 8
LOAD_TILE = 9
EARLY_TILE = 6
LATE_TILE = 9

EPS_SCALE = 0.1
NU_BASE = 0.02
TAU_STAB = 1.0
SENSOR_MID = -2.0
SENSOR_WIDTH = 0.5
RATIO_FLOOR = 0.0001

F32 = jnp.float32
BF16 = jnp.bfloat16
I32 = jnp.int32
MESH = pl.DeviceIdType.MESH
NN = (((1,), (0,)), ((), ()))
NT = (((1,), (1,)), ((), ()))
VMEM_LIMIT = 60 * 1024 * 1024


def iota(shape, axis):
    return lax.broadcasted_iota(I32, shape, axis)


def split3(x):
    high = x.astype(BF16)
    rest = x - high.astype(F32)
    middle = rest.astype(BF16)
    low = (rest - middle.astype(F32)).astype(BF16)
    return high, middle, low


def split2(x):
    high = x.astype(BF16)
    return high, (x - high.astype(F32)).astype(BF16)


def dot(a, b, dims):
    return lax.dot_general(a, b, dims, preferred_element_type=F32)


def one_hot(mask):
    return jnp.where(mask, 1.0, 0.0).astype(BF16)


def element_eps(density, speed, flags):
    ids = iota((MODES, LANES), 0)
    degree = jnp.maximum(jnp.maximum(ids >> 4, (ids >> 2) & 3), ids & 3)
    squares = density * density
    totals = jnp.sum(squares, axis=0, keepdims=True) + 1e-06
    high = jnp.sum(jnp.where(degree == 3, squares, 0.0), axis=0, keepdims=True)
    sensor = jnp.log10(jnp.maximum(high / totals, RATIO_FLOOR))
    ramped = 0.5 * (1.0 + jnp.tanh((sensor - SENSOR_MID) / SENSOR_WIDTH))
    return EPS_SCALE * speed * jnp.maximum(ramped, 0.5 * flags.astype(F32))


def padded_row(row):
    source = (row * 2731) >> 16
    return source, row - source * CAP


def partner_rows(face_ref):
    pieces = [
        face_ref[end : end + 1, chunk * LANES : (chunk + 1) * LANES]
        for end in range(2)
        for chunk in range(6)
    ]
    stacked = jnp.concatenate(pieces + [jnp.zeros((LANES - 12, LANES), I32)], axis=0)
    turned = jnp.transpose(stacked.astype(F32)).astype(I32)
    high_parts = []
    low_parts = []
    for end in range(2):
        own_p, own_i = padded_row(face_ref[end : end + 1, :])
        other_p, other_i = padded_row(face_ref[1 - end : 2 - end, :])
        mine = iota((16, FACES), 0) == (own_p >> 2)
        high_parts.append(
            jnp.concatenate(
                [
                    jnp.where(mine, other_p.astype(F32), 0.0),
                    jnp.where(mine, other_i.astype(F32), 0.0),
                ],
                axis=0,
            ).astype(BF16)
        )
        columns = []
        for chunk in range(6):
            n = end * 6 + chunk
            col_p, col_i = padded_row(turned[:, n : n + 1])
            place = ((col_p & 3) << 5) + col_i
            columns.append(one_hot(iota((LANES, LANES), 1) == place))
        low_parts.append(jnp.concatenate(columns, axis=0))
    found = dot(high_parts[0], low_parts[0], NN) + dot(high_parts[1], low_parts[1], NN)
    found = found.astype(I32)
    return found[0:16], found[16:32]


def remote(src, dst, send_sem, recv_sem, where):
    return pltpu.make_async_remote_copy(
        src_ref=src,
        dst_ref=dst,
        send_sem=send_sem,
        recv_sem=recv_sem,
        device_id=where,
        device_id_type=MESH,
    )


def block_row(i, j):
    d = (i - j) % 8
    if i >= 8 > j:
        return 64 + d * 8 + j
    base = 32 if j >= 8 else 0
    low, high = j % 8, i % 8
    if d < 4:
        return base + d * 8 + low
    if d > 4:
        return base + (8 - d) * 8 + high
    return 128 + (high if base else low)


def multiply_blocks(coupling_ref, products):
    sub = iota((8, LANES), 0)

    def body(k, carry):
        for j in range(EFACES):
            c = coupling_ref[k, j * FNODES : (j + 1) * FNODES, :].astype(F32)
            c0, c1 = c[0:8], c[8:16]
            turned = [c1] + [pltpu.roll(c1, 8 - d, 0) for d in range(1, 8)]
            for d in range(4):
                products[j, k, d * 8 : d * 8 + 8, :] = c0 * (pltpu.roll(c0, 8 - d, 0) if d else c0)
                products[j, k, 32 + d * 8 : 40 + d * 8, :] = c1 * turned[d]
            for d in range(8):
                products[j, k, 64 + d * 8 : 72 + d * 8, :] = c0 * turned[d]
            products[j, k, 128:136, :] = jnp.where(
                sub < 4, c0 * pltpu.roll(c0, 4, 0), c1 * turned[4]
            )
        return carry

    lax.fori_loop(0, MODES, body, 0)


def condense_blocks(coef_ref, products, parts_a, pay_b):
    for j in range(EFACES):

        def body(k, sums):
            return sums + coef_ref[pl.ds(k, 1), :] * products[j, k]

        row = iota((TRI, LANES), 0)
        diagonal = jnp.logical_or(row < 8, jnp.logical_and(row >= 32, row < 40))
        start = jnp.where(diagonal, TAU_STAB, 0.0)
        sums = lax.fori_loop(0, MODES, body, start, unroll=8)
        at = pl.ds(j * LANES, LANES)
        parts_a[:, at] = jnp.concatenate(split3(sums[0:LANES]), axis=0)
        pay_b[pl.ds(0, 8), at] = sums[LANES:TRI]


def condense_loads(weighted_ref, coupling_ref, face_ref, pay_b):
    for j in range(EFACES):

        def body(k, sums):
            c = coupling_ref[k, j * FNODES : (j + 1) * FNODES, :].astype(F32)
            return tuple(
                sums[comp] + c * weighted_ref[comp, pl.ds(k, 1), :] for comp in range(COMPS)
            )

        start = (jnp.zeros((FNODES, LANES), F32),) * COMPS
        sums = lax.fori_loop(0, MODES, body, start, unroll=8)
        at = pl.ds(j * LANES, LANES)
        for comp in range(COMPS):
            pay_b[pl.ds(8 + comp * FNODES, FNODES), at] = (
                face_ref[comp, j * FNODES : (j + 1) * FNODES, :] - sums[comp]
            )
        pay_b[pl.ds(88, LANES - 88), at] = jnp.zeros((LANES - 88, LANES), F32)


def pick(hot, parts):
    found = dot(hot, parts, NT)
    return found[:, 0:LANES] + found[:, LANES : 2 * LANES] + found[:, 2 * LANES :]


def pack_first(x0, x1, x2, out_ref, q):
    lane = iota((8, LANES), 1)
    out_ref[q] = jnp.where(
        lane < 40, x0, jnp.where(lane < 80, pltpu.roll(x1, 40, 1), pltpu.roll(x2, 80, 1))
    )


def unpack_first(tile):
    lane = iota((8, LANES), 1)
    zero = jnp.zeros((8, LANES), F32)
    return [
        jnp.where(lane < 40, x, zero) for x in (tile, pltpu.roll(tile, 88, 1), pltpu.roll(tile, 48, 1))
    ]


def pack48(x0, x1, x2, out_ref, q):
    lane = iota((8, LANES), 1)
    sub = iota((8, LANES), 0)
    turned = pltpu.roll(x2, 96, 1)
    out_ref[q, 0:8, :] = jnp.where(
        lane < 48, x0, jnp.where(lane < 96, pltpu.roll(x1, 48, 1), turned)
    )
    spread = pltpu.roll(turned, 0, 1, stride=16, stride_axis=0)
    out_ref[q, 8:9, :] = jnp.sum(jnp.where((lane >> 4) == sub, spread, 0.0), axis=0, keepdims=True)


def unpack48(tile, tail):
    lane = iota((8, LANES), 1)
    sub = iota((8, LANES), 0)
    zero = jnp.zeros((8, LANES), F32)
    spread = pltpu.roll(jnp.broadcast_to(tail, (8, LANES)), 48, 1)
    spread = pltpu.roll(spread, 0, 1, stride=16, stride_axis=0)
    spread = jnp.take_along_axis(spread, 7 - sub, axis=0)
    return [
        jnp.where(lane < 48, tile, zero),
        jnp.where(lane < 48, pltpu.roll(tile, 80, 1), zero),
        jnp.where(lane < 32, pltpu.roll(tile, 32, 1), jnp.where(lane < 48, spread, zero)),
    ]


def pack32(x0, x1, x2, out_ref, q):
    lane = iota((8, LANES), 1)
    sub = iota((8, LANES), 0)
    full = jnp.where(
        lane < 32, x0, jnp.where(lane < 64, pltpu.roll(x1, 32, 1), pltpu.roll(x2, 64, 1))
    )
    extra = jnp.zeros((8, LANES), F32)
    for c in range(3):
        turned = pltpu.roll(full, 96 - 32 * c, 1)
        extra = jnp.where(sub == c, jnp.broadcast_to(turned[6:7], (8, LANES)), extra)
        extra = jnp.where(sub == 3 + c, jnp.broadcast_to(turned[7:8], (8, LANES)), extra)
    out_ref[q] = jnp.where(lane < 96, full, extra)[0:6]


def unpack32(tile):
    lane = iota((8, LANES), 1)
    sub = iota((8, LANES), 0)
    zero = jnp.zeros((8, LANES), F32)
    full = jnp.concatenate([tile, zero[0:2]], axis=0)
    turned = [pltpu.roll(full, 32 * c + 32, 1) for c in range(3)]
    one = lane[0:1]
    for r in range(2):
        row = jnp.where(
            one < 32,
            turned[0][3 * r : 3 * r + 1],
            jnp.where(one < 64, turned[1][3 * r + 1 : 3 * r + 2], turned[2][3 * r + 2 : 3 * r + 3]),
        )
        full = jnp.where(sub == 6 + r, jnp.broadcast_to(row, (8, LANES)), full)
    return [
        jnp.where(lane < 32, x, zero) for x in (full, pltpu.roll(full, 96, 1), pltpu.roll(full, 64, 1))
    ]


def thirds(x):
    return x[0:8], x[8:16], x[16:24]


def lower_row(i, k):
    return k * FNODES - k * (k - 1) // 2 + i - k


def factor_faces(grid, idle, lower_ref, inverse_ref):
    scaled = []
    lower = []
    for j in range(FNODES):
        column = jnp.stack([grid[block_row(i, j)] for i in range(j, FNODES)], axis=0)
        for k in range(j):
            column = column - scaled[k][j - k :] * lower[k][j - k][None]
        pivot = 1.0 / (column[0] + idle)
        inverse_ref[j] = pivot
        scaled.append(column)
        lower.append(column * pivot[None])
        lower_ref[lower_row(j, j) : lower_row(j, j) + FNODES - j] = lower[j]


def solve_faces(grid, lower_ref, inverse_ref, comps, answer):
    forward = []
    for i in range(FNODES):
        total = jnp.stack([grid[TRI + comp * FNODES + i] for comp in comps], axis=0)
        for k in range(i):
            total = total - lower_ref[lower_row(i, k)][None] * forward[k]
        forward.append(total)
    solved = [None] * FNODES
    for i in reversed(range(FNODES)):
        total = forward[i] * inverse_ref[i][None]
        for k in range(i + 1, FNODES):
            total = total - lower_ref[lower_row(k, i)][None] * solved[k]
        solved[i] = total
        for n, comp in enumerate(comps):
            answer[comp * FNODES + i] = total[n]


def ring_offset(n):
    t = N_Z - 1 - n
    half = lax.div(t + 1, 2)
    return lax.rem(16 + half * (2 * lax.rem(t, 2) - 1), 16)


def spread_slots(lists, slots):
    lane = iota((4, LANES), 1)
    rows = [lists[pl.ds(a, 4, stride=3), :] for a in range(3)]
    for z in range(N_Z):
        a, b = divmod(z * CAP, LANES)
        value = pltpu.roll(rows[a], LANES - b, 1) if b else rows[a]
        if b + CAP > LANES:
            value = jnp.where(lane < LANES - b, value, pltpu.roll(rows[a + 1], LANES - b, 1))
        slots[pl.ds(z, 4, stride=N_Z), :] = jnp.where(lane < CAP, value, SLOTS)


def step_kernel(
    density_hbm,
    speed_hbm,
    flags_hbm,
    mass_hbm,
    eigs_hbm,
    send_hbm,
    face_hbm,
    coupling_hbm,
    inner_hbm,
    faceres_hbm,
    traces_ref,
    coef_ref,
    density,
    speed_ref,
    flags,
    mass,
    eigs_ref,
    lists,
    face_ref,
    coupling,
    inner,
    faceres,
    slots_ref,
    weighted,
    eps_out,
    eps_in,
    visc_out,
    visc_in,
    top_out,
    tops,
    slot_hot,
    row_hot,
    products,
    masks,
    pay_b,
    parts_a,
    parts_b,
    rows,
    whole_out,
    whole_in,
    first_out,
    first_in,
    loads_out,
    loads_in,
    joined_a,
    joined_b,
    grid,
    lower,
    inverse,
    answer,
    early_out,
    early_in,
    late_out,
    late_in,
    load_sem,
    send_a,
    recv_a,
    send_b,
    recv_b,
    send_c,
    recv_c,
    send_d,
    recv_d,
    send_e,
    recv_e,
    send_f,
    recv_f,
    send_g,
    recv_g,
    send_h,
    recv_h,
):
    me = lax.axis_index("dom")
    group = lax.axis_index("group")
    my_y = lax.div(me, N_Z)
    my_z = lax.rem(me, N_Z)
    following = {"dom": lax.rem(me + 1, N_DOM)}
    barrier = pltpu.get_barrier_semaphore()

    def each_peer(act):
        def one_z(n, carry):
            z = lax.rem(my_z + ring_offset(n), N_Z)
            for dy in (2, 1, 3, 0):
                act(lax.rem(my_y + dy, N_Y) * N_Z + z)
            return carry

        lax.fori_loop(0, N_Z - 1, one_z, 0)
        for dy in (2, 1, 3):
            act(lax.rem(my_y + dy, N_Y) * N_Z + my_z)

    def each_group(act):
        def one(k, carry):
            act(lax.rem(group + k, N_GROUP))
            return carry

        lax.fori_loop(1, N_GROUP, one, 0)

    each_peer(
        lambda q: pl.semaphore_signal(barrier, inc=1, device_id={"dom": q}, device_id_type=MESH)
    )
    each_group(
        lambda g: pl.semaphore_signal(barrier, inc=1, device_id={"group": g}, device_id_type=MESH)
    )
    loads = [
        pltpu.make_async_copy(source, target, load_sem.at[n])
        for n, (source, target) in enumerate(
            (
                (density_hbm, density),
                (speed_hbm, speed_ref),
                (flags_hbm, flags),
                (send_hbm, lists),
                (face_hbm, face_ref),
                (coupling_hbm, coupling),
                (mass_hbm, mass),
                (eigs_hbm, eigs_ref),
                (inner_hbm, inner),
                (faceres_hbm, faceres),
            )
        )
    ]
    for copy in loads:
        copy.start()
    for copy in loads[:5]:
        copy.wait()

    speed = speed_ref[...]
    eps = element_eps(density[...], speed, flags[...])
    spread_slots(lists, slots_ref)
    slots = slots_ref[...]
    lane = iota((N_DOM, LANES), 1)
    values = jnp.take_along_axis(
        jnp.broadcast_to(eps, (N_DOM, LANES)), slots & (ELEM_DEV - 1), axis=1
    )
    values = jnp.where(slots < SLOTS, values, 0.0)
    values = jnp.where(lane == LANES - 1, jnp.max(speed, axis=1, keepdims=True), values)
    for q in range(N_DOM):
        eps_out[q] = values[q : q + 1, :]

    for y in range(N_Y):
        for i in range(CAP):
            column = slots[y * N_Z : (y + 1) * N_Z, i : i + 1]
            slot_hot[y, i * N_Z : (i + 1) * N_Z, :] = one_hot(iota((N_Z, SLOTS), 1) == column)

    pl.semaphore_wait(barrier, N_DOM + N_GROUP - 2)
    each_peer(
        lambda q: remote(eps_out.at[q], eps_in.at[me], send_a, recv_a, {"dom": q}).start()
    )
    eps_in[me] = eps_out[me]
    partner_p, partner_i = partner_rows(face_ref)
    loads[5].wait()
    multiply_blocks(coupling, products)
    others = pl.ds(0, N_DOM - 1)
    whole = remote(eps_out.at[others], eps_in.at[others], send_a, recv_a, following)
    whole.wait_recv()
    whole.wait_send()

    partner_eps = jnp.zeros((16, LANES), F32)
    top = jnp.zeros((1, LANES), F32)
    for p in range(N_DOM):
        row = eps_in[p]
        top = jnp.maximum(top, row)
        found = jnp.take_along_axis(jnp.broadcast_to(row, (16, LANES)), partner_i, axis=1)
        partner_eps = jnp.where(partner_p == p, found, partner_eps)
    for r in range(16):
        visc_out[r] = partner_eps[r : r + 1, :]
    top_out[0] = top
    each_peer(
        lambda p: remote(
            visc_out.at[lax.div(p, 4)], visc_in.at[me], send_b, recv_b, {"dom": p}
        ).start()
    )
    each_group(
        lambda g: remote(top_out.at[0], tops.at[group], send_c, recv_c, {"group": g}).start()
    )
    visc_in[me] = visc_out[lax.div(me, 4)]
    tops[group] = top_out[0]

    for y in range(N_Y):
        received = iota((PART, FACES), 0) + y * PART
        row_hot[y] = one_hot(
            jnp.logical_or(received == face_ref[0:1, :], received == face_ref[1:2, :])
        )
    for i in range(CAP):
        slot = slots[:, i : i + 1]
        here = jnp.logical_and((slot & (ELEM_DEV - 1)) == lane, slot < SLOTS)
        masks[i] = jnp.where(here, 1.0, 0.0)
    for copy in loads[6:]:
        copy.wait()

    whole = remote(eps_in.at[others], visc_in.at[others], send_b, recv_b, following)
    whole.wait_recv()
    whole.wait_send()
    seven = pl.ds(0, N_GROUP - 1)
    whole = remote(
        tops.at[seven],
        tops.at[seven],
        send_c,
        recv_c,
        {"group": lax.rem(group + 1, N_GROUP)},
    )
    whole.wait_recv()
    whole.wait_send()

    came = jnp.concatenate([visc_in[q] for q in range(N_DOM)], axis=0)
    came = pltpu.roll(came, lax.rem(4 - lax.rem(me, 4), 4) * 32, 1)
    total = jnp.zeros((N_DOM, LANES), F32)
    for i in range(CAP):
        total = total + masks[i] * came[:, i : i + 1]
    gathered = jnp.sum(total, axis=0, keepdims=True)
    nu = NU_BASE + (EFACES * eps + gathered) / (2.0 * EFACES)
    top = tops[0]
    for g in range(1, N_GROUP):
        top = jnp.maximum(top, tops[g])
    peak = jnp.max(jnp.where(iota((1, LANES), 1) == LANES - 1, top, 0.0), axis=1, keepdims=True)
    square = iota((MODES, MODES), 0) == iota((MODES, MODES), 1)
    eigs = jnp.sum(jnp.where(square, eigs_ref[...], 0.0), axis=1, keepdims=True)
    coef = 1.0 / (mass[...] * (1.0 + speed / peak + nu * eigs))
    coef_ref[...] = coef

    condense_blocks(coef_ref, products, parts_a, pay_b)
    for c in range(N_Y):
        y = lax.rem(my_y + c, N_Y)
        rows[...] = pick(slot_hot[y], parts_a[...])

        def send_whole(n, carry):
            z = lax.rem(my_z + ring_offset(n), N_Z)
            q = y * N_Z + z
            whole_out[q] = rows[pl.ds(z, CAP, stride=16), :]
            remote(whole_out.at[q], whole_in.at[me], send_d, recv_d.at[c], {"dom": q}).start()
            return carry

        lax.fori_loop(0, N_Z if c else N_Z - 1, send_whole, 0)
        if c == 0:
            whole_in[me] = rows[pl.ds(my_z, CAP, stride=16), :]
    weighted[...] = inner[...] * coef[None]
    condense_loads(weighted, coupling, faceres, pay_b)
    parts_b[...] = jnp.concatenate(split3(pay_b[...]), axis=0)
    for c in range(N_Y):
        y = lax.rem(my_y + c, N_Y)
        rows[...] = pick(slot_hot[y], parts_b[...])

        def pack_rest(z, first_ref, loads_ref, q):
            rest = rows[pl.ds(z, CAP, stride=16), :]
            pack_first(*thirds(rest), first_ref, q)
            pack48(*thirds(pltpu.roll(rest, 88, 1)), loads_ref, q)

        def send_rest(n, carry):
            z = lax.rem(my_z + ring_offset(n), N_Z)
            q = y * N_Z + z
            pack_rest(z, first_out, loads_out, q)
            remote(first_out.at[q], first_in.at[me], send_e, recv_e.at[c], {"dom": q}).start()
            return carry

        lax.fori_loop(0, N_Z if c else N_Z - 1, send_rest, 0)
        if c == 0:
            pack_rest(my_z, first_in, loads_in, me)
    for c in range(N_Y):
        y = lax.rem(my_y + c, N_Y)

        def send_loads(n, carry):
            q = y * N_Z + lax.rem(my_z + ring_offset(n), N_Z)
            remote(loads_out.at[q], loads_in.at[me], send_g, recv_g.at[c], {"dom": q}).start()
            return carry

        lax.fori_loop(0, N_Z if c else N_Z - 1, send_loads, 0)

    def to_grid(joined, start, height):
        for chunk in range(6):
            for n in range(height // 8):
                grid[start + n * 8 : start + n * 8 + 8, chunk, :] = joined[
                    n * 8 : n * 8 + 8, chunk * LANES : (chunk + 1) * LANES
                ]

    for c in range(N_Y):
        y = lax.rem(my_y + N_Y - c, N_Y)
        sources = pl.ds(0, N_Z if c else N_Z - 1)
        remote(
            whole_out.at[sources], whole_in.at[sources], send_d, recv_d.at[c], following
        ).wait_recv()
        came = whole_in[pl.ds(pl.multiple_of(y * N_Z, N_Z), N_Z)].reshape(PART, LANES)
        stacked = jnp.concatenate(split3(jnp.transpose(came)), axis=0)
        found = dot(stacked, row_hot[y], NN)
        found = found[0:LANES] + found[LANES : 2 * LANES] + found[2 * LANES :]
        joined_a[...] = found if c == 0 else joined_a[...] + found
    to_grid(joined_a, 0, LANES)
    remote(whole_out.at[others], whole_in.at[others], send_d, recv_d.at[0], following).wait_send()

    def take_rest(out_ref, in_ref, send_sem, recv_sem, unpack):
        for c in range(N_Y):
            y = lax.rem(my_y + N_Y - c, N_Y)
            sources = pl.ds(0, N_Z if c else N_Z - 1)
            remote(
                out_ref.at[sources], in_ref.at[sources], send_sem, recv_sem.at[c], following
            ).wait_recv()

            def take(z, carry):
                base = pl.multiple_of(z * CAP, 8)
                rows[pl.ds(base, CAP), :] = jnp.concatenate(unpack(y * N_Z + z), axis=0)
                return carry

            lax.fori_loop(0, N_Z, take, 0, unroll=2)
            stacked = jnp.concatenate(split3(jnp.transpose(rows[...])[0:HALF]), axis=0)
            found = dot(stacked, row_hot[y], NN)
            found = found[0:HALF] + found[HALF : 2 * HALF] + found[2 * HALF :]
            joined_b[...] = found if c == 0 else joined_b[...] + found
        remote(out_ref.at[others], in_ref.at[others], send_sem, recv_sem.at[0], following).wait_send()

    def send_back(comps, pack, out_ref, in_ref, send_sem, recv_sem):
        start, height = comps[0] * FNODES, len(comps) * FNODES
        face_traces = jnp.concatenate(
            [answer[start : start + height, chunk, :] for chunk in range(6)], axis=1
        )
        gap = jnp.zeros((LANES - height, FACES), BF16)
        high, low = split2(face_traces)
        both = jnp.concatenate([high, gap, low, gap], axis=0)
        for c in range(N_Y):
            y = lax.rem(my_y + c, N_Y)
            found = dot(row_hot[y], both, NT)
            rows[...] = found[:, 0:LANES] + found[:, LANES : 2 * LANES]

            def send(n, carry):
                z = lax.rem(my_z + ring_offset(n), N_Z)
                p = y * N_Z + z
                base = pl.multiple_of(z * CAP, 8)
                pack(*thirds(rows[pl.ds(base, CAP), :]), out_ref, p)
                remote(out_ref.at[p], in_ref.at[me], send_sem, recv_sem.at[c], {"dom": p}).start()
                return carry

            lax.fori_loop(0, N_Z if c else N_Z - 1, send, 0)
            if c == 0:
                base = pl.multiple_of(my_z * CAP, 8)
                pack(*thirds(rows[pl.ds(base, CAP), :]), in_ref, me)

    def take_traces(comps, unpack, out_ref, in_ref, send_sem, recv_sem):
        height = len(comps) * FNODES
        for c in range(N_Y):
            y = lax.rem(my_y + N_Y - c, N_Y)
            sources = pl.ds(0, N_Z if c else N_Z - 1)
            remote(
                out_ref.at[sources], in_ref.at[sources], send_sem, recv_sem.at[c], following
            ).wait_recv()

            def take(z, carry):
                rows[pl.ds(z, CAP, stride=16), :] = jnp.concatenate(unpack(y * N_Z + z), axis=0)
                return carry

            lax.fori_loop(0, N_Z, take, 0, unroll=2)
            turned = jnp.transpose(rows[...])[0:height]
            found = dot(jnp.concatenate(split2(turned), axis=0), slot_hot[y], NN)
            found = found[0:height] + found[height:]
            for n, comp in enumerate(comps):
                for j in range(EFACES):
                    piece = found[n * FNODES : (n + 1) * FNODES, j * LANES : (j + 1) * LANES]
                    at = slice(j * FNODES, (j + 1) * FNODES)
                    traces_ref[comp, at, :] = piece if c == 0 else traces_ref[comp, at, :] + piece
        remote(out_ref.at[others], in_ref.at[others], send_sem, recv_sem.at[0], following).wait_send()

    early = tuple(range(EARLY))
    late = tuple(range(EARLY, COMPS))
    take_rest(first_out, first_in, send_e, recv_e, lambda p: unpack_first(first_in[p]))
    to_grid(joined_b, LANES, 40)
    first = face_ref[0:1, :]
    idle = jnp.concatenate(
        [first[:, chunk * LANES : (chunk + 1) * LANES] for chunk in range(6)]
        + [jnp.full((2, LANES), ROWS, I32)],
        axis=0,
    )
    factor_faces(grid, jnp.where(idle < ROWS, 0.0, 1.0), lower, inverse)
    solve_faces(grid, lower, inverse, early, answer)
    send_back(early, pack32, early_out, early_in, send_f, recv_f)
    take_rest(
        loads_out,
        loads_in,
        send_g,
        recv_g,
        lambda p: unpack48(loads_in[p, 0:8, :], loads_in[p, 8:9, :]),
    )
    to_grid(joined_b, LANES + 40, HALF)
    solve_faces(grid, lower, inverse, late, answer)
    send_back(late, pack48, late_out, late_in, send_h, recv_h)
    take_traces(early, lambda q: unpack32(early_in[q]), early_out, early_in, send_f, recv_f)
    take_traces(
        late,
        lambda q: unpack48(late_in[q, 0:8, :], late_in[q, 8:9, :]),
        late_out,
        late_in,
        send_h,
        recv_h,
    )


def update_kernel(traces_in, coef_ref, coupling_ref, inner_ref, update_ref, traces_ref):
    traces_ref[...] = traces_in[...]

    def substitute(k, carry):
        c = coupling_ref[k].astype(F32)
        coef = coef_ref[pl.ds(k, 1), :]
        for comp in range(COMPS):
            pulled = jnp.sum(c * traces_in[comp], axis=0, keepdims=True)
            update_ref[comp, pl.ds(k, 1), :] = coef * (inner_ref[comp, pl.ds(k, 1), :] - pulled)
        return carry

    lax.fori_loop(0, MODES, substitute, 0, unroll=4)


def local(
    density_modes,
    wave_speed,
    shock_flags,
    elem_mass,
    stiff_eigs,
    coupling,
    interior_res,
    face_res,
    send_rows,
    face_rows,
):
    vmem = pl.BlockSpec(memory_space=pltpu.VMEM)
    anywhere = pl.BlockSpec(memory_space=pltpu.HBM)
    dma = pltpu.SemaphoreType.DMA
    traces, coef = pl.pallas_call(
        step_kernel,
        out_shape=(
            pltpu.VMEM((COMPS, TRACE, LANES), F32),
            pltpu.VMEM((MODES, LANES), F32),
        ),
        in_specs=[anywhere] * 10,
        out_specs=(vmem, vmem),
        scratch_shapes=[
            pltpu.VMEM((MODES, LANES), F32),
            pltpu.VMEM((1, LANES), F32),
            pltpu.VMEM((1, LANES), I32),
            pltpu.VMEM((1, LANES), F32),
            pltpu.VMEM((1, MODES), F32),
            pltpu.VMEM((12, LANES), I32),
            pltpu.VMEM((2, FACES), I32),
            pltpu.VMEM((MODES, TRACE, LANES), BF16),
            pltpu.VMEM((COMPS, MODES, LANES), F32),
            pltpu.VMEM((COMPS, TRACE, LANES), F32),
            pltpu.VMEM((N_DOM, LANES), I32),
            pltpu.VMEM((COMPS, MODES, LANES), F32),
            pltpu.VMEM((N_DOM, 1, LANES), F32),
            pltpu.VMEM((N_DOM, 1, LANES), F32),
            pltpu.VMEM((16, 1, LANES), F32),
            pltpu.VMEM((N_DOM, 1, LANES), F32),
            pltpu.VMEM((1, 1, LANES), F32),
            pltpu.VMEM((N_GROUP, 1, LANES), F32),
            pltpu.VMEM((N_Y, PART, SLOTS), BF16),
            pltpu.VMEM((N_Y, PART, FACES), BF16),
            pltpu.VMEM((EFACES, MODES, TRI, LANES), F32),
            pltpu.VMEM((CAP, N_DOM, LANES), F32),
            pltpu.VMEM((LANES, SLOTS), F32),
            pltpu.VMEM((3 * LANES, SLOTS), BF16),
            pltpu.VMEM((3 * LANES, SLOTS), BF16),
            pltpu.VMEM((PART, LANES), F32),
            pltpu.VMEM((N_DOM, CAP, LANES), F32),
            pltpu.VMEM((N_DOM, CAP, LANES), F32),
            pltpu.VMEM((N_DOM, FIRST_TILE, LANES), F32),
            pltpu.VMEM((N_DOM, FIRST_TILE, LANES), F32),
            pltpu.VMEM((N_DOM, LOAD_TILE, LANES), F32),
            pltpu.VMEM((N_DOM, LOAD_TILE, LANES), F32),
            pltpu.VMEM((LANES, FACES), F32),
            pltpu.VMEM((HALF, FACES), F32),
            pltpu.VMEM((USED, 8, LANES), F32),
            pltpu.VMEM((TRI, 8, LANES), F32),
            pltpu.VMEM((FNODES, 8, LANES), F32),
            pltpu.VMEM((COMPS * FNODES, 8, LANES), F32),
            pltpu.VMEM((N_DOM, EARLY_TILE, LANES), F32),
            pltpu.VMEM((N_DOM, EARLY_TILE, LANES), F32),
            pltpu.VMEM((N_DOM, LATE_TILE, LANES), F32),
            pltpu.VMEM((N_DOM, LATE_TILE, LANES), F32),
            dma((10,)),
            dma,
            dma,
            dma,
            dma,
            dma,
            dma,
            dma,
            dma((N_Y,)),
            dma,
            dma((N_Y,)),
            dma,
            dma((N_Y,)),
            dma,
            dma((N_Y,)),
            dma,
            dma((N_Y,)),
        ],
        compiler_params=pltpu.CompilerParams(
            collective_id=0, has_side_effects=True, vmem_limit_bytes=VMEM_LIMIT
        ),
        name="newton_step",
    )(
        density_modes,
        wave_speed[None, :],
        shock_flags[None, :],
        elem_mass[None, :],
        stiff_eigs[None, :],
        send_rows.reshape(12, LANES),
        face_rows,
        coupling,
        interior_res,
        face_res,
    )
    return pl.pallas_call(
        update_kernel,
        out_shape=(
            jax.ShapeDtypeStruct((COMPS, MODES, LANES), F32),
            jax.ShapeDtypeStruct((COMPS, TRACE, LANES), F32),
        ),
        in_specs=[vmem] * 4,
        out_specs=(vmem, vmem),
        compiler_params=pltpu.CompilerParams(vmem_limit_bytes=16 * 1024 * 1024),
        name="back_substitute",
    )(traces, coef, coupling, interior_res)


def solution(mesh):
    return jax.shard_map(
        local,
        mesh=mesh,
        in_specs=(
            P(None, ("group", "dom")),
            P(("group", "dom")),
            P(("group", "dom")),
            P(("group", "dom")),
            P(),
            P(None, None, ("group", "dom")),
            P(None, None, ("group", "dom")),
            P(None, None, ("group", "dom")),
            P(("group", "dom")),
            P(None, ("group", "dom")),
        ),
        out_specs=(P(None, None, ("group", "dom")), P(None, None, ("group", "dom"))),
        check_vma=False,
    )
```

```python
import jax
import jax.numpy as jnp
from jax import lax
from jax.experimental import pallas as pl
from jax.experimental.pallas import tpu as pltpu
from jax.sharding import PartitionSpec as P

MODES = 64
FNODES = 16
COMPS = 5
EFACES = 6
TRACE = 96
ELEM_DEV = 128
SLOTS = EFACES * ELEM_DEV
CAP = 24
N_DOM = 64
N_GROUP = 8
ROWS = N_DOM * CAP
FACES = 768
TRI = 136
USED = 216
N_Z = 16
N_Y = N_DOM // N_Z
PART = N_Z * CAP
LANES = 128
HALF = 96
REST_TILE = 17
RET_TILE = 15

EPS_SCALE = 0.1
NU_BASE = 0.02
TAU_STAB = 1.0
SENSOR_MID = -2.0
SENSOR_WIDTH = 0.5
RATIO_FLOOR = 0.0001

F32 = jnp.float32
BF16 = jnp.bfloat16
I32 = jnp.int32
MESH = pl.DeviceIdType.MESH
NN = (((1,), (0,)), ((), ()))
NT = (((1,), (1,)), ((), ()))
VMEM_LIMIT = 60 * 1024 * 1024


def iota(shape, axis):
    return lax.broadcasted_iota(I32, shape, axis)


def split3(x):
    high = x.astype(BF16)
    rest = x - high.astype(F32)
    middle = rest.astype(BF16)
    low = (rest - middle.astype(F32)).astype(BF16)
    return high, middle, low


def split2(x):
    high = x.astype(BF16)
    return high, (x - high.astype(F32)).astype(BF16)


def dot(a, b, dims):
    return lax.dot_general(a, b, dims, preferred_element_type=F32)


def one_hot(mask):
    return jnp.where(mask, 1.0, 0.0).astype(BF16)


def element_eps(density, speed, flags):
    ids = iota((MODES, LANES), 0)
    degree = jnp.maximum(jnp.maximum(ids >> 4, (ids >> 2) & 3), ids & 3)
    squares = density * density
    totals = jnp.sum(squares, axis=0, keepdims=True) + 1e-06
    high = jnp.sum(jnp.where(degree == 3, squares, 0.0), axis=0, keepdims=True)
    sensor = jnp.log10(jnp.maximum(high / totals, RATIO_FLOOR))
    ramped = 0.5 * (1.0 + jnp.tanh((sensor - SENSOR_MID) / SENSOR_WIDTH))
    return EPS_SCALE * speed * jnp.maximum(ramped, 0.5 * flags.astype(F32))


def padded_row(row):
    source = (row * 2731) >> 16
    return source, row - source * CAP


def partner_rows(face_ref):
    pieces = [
        face_ref[end : end + 1, chunk * LANES : (chunk + 1) * LANES]
        for end in range(2)
        for chunk in range(6)
    ]
    stacked = jnp.concatenate(pieces + [jnp.zeros((LANES - 12, LANES), I32)], axis=0)
    turned = jnp.transpose(stacked.astype(F32)).astype(I32)
    high_parts = []
    low_parts = []
    for end in range(2):
        own_p, own_i = padded_row(face_ref[end : end + 1, :])
        other_p, other_i = padded_row(face_ref[1 - end : 2 - end, :])
        mine = iota((16, FACES), 0) == (own_p >> 2)
        high_parts.append(
            jnp.concatenate(
                [
                    jnp.where(mine, other_p.astype(F32), 0.0),
                    jnp.where(mine, other_i.astype(F32), 0.0),
                ],
                axis=0,
            ).astype(BF16)
        )
        columns = []
        for chunk in range(6):
            n = end * 6 + chunk
            col_p, col_i = padded_row(turned[:, n : n + 1])
            place = ((col_p & 3) << 5) + col_i
            columns.append(one_hot(iota((LANES, LANES), 1) == place))
        low_parts.append(jnp.concatenate(columns, axis=0))
    found = dot(high_parts[0], low_parts[0], NN) + dot(high_parts[1], low_parts[1], NN)
    found = found.astype(I32)
    return found[0:16], found[16:32]


def remote(src, dst, send_sem, recv_sem, where):
    return pltpu.make_async_remote_copy(
        src_ref=src,
        dst_ref=dst,
        send_sem=send_sem,
        recv_sem=recv_sem,
        device_id=where,
        device_id_type=MESH,
    )


def block_row(i, j):
    d = (i - j) % 8
    if i >= 8 > j:
        return 64 + d * 8 + j
    base = 32 if j >= 8 else 0
    low, high = j % 8, i % 8
    if d < 4:
        return base + d * 8 + low
    if d > 4:
        return base + (8 - d) * 8 + high
    return 128 + (high if base else low)


def multiply_blocks(coupling_ref, products):
    sub = iota((8, LANES), 0)

    def body(k, carry):
        for j in range(EFACES):
            c = coupling_ref[k, j * FNODES : (j + 1) * FNODES, :].astype(F32)
            c0, c1 = c[0:8], c[8:16]
            turned = [c1] + [pltpu.roll(c1, 8 - d, 0) for d in range(1, 8)]
            for d in range(4):
                products[j, k, d * 8 : d * 8 + 8, :] = c0 * (pltpu.roll(c0, 8 - d, 0) if d else c0)
                products[j, k, 32 + d * 8 : 40 + d * 8, :] = c1 * turned[d]
            for d in range(8):
                products[j, k, 64 + d * 8 : 72 + d * 8, :] = c0 * turned[d]
            products[j, k, 128:136, :] = jnp.where(
                sub < 4, c0 * pltpu.roll(c0, 4, 0), c1 * turned[4]
            )
        return carry

    lax.fori_loop(0, MODES, body, 0)


def condense_blocks(coef_ref, products, parts_a, pay_b):
    for j in range(EFACES):

        def body(k, sums):
            return sums + coef_ref[pl.ds(k, 1), :] * products[j, k]

        row = iota((TRI, LANES), 0)
        diagonal = jnp.logical_or(row < 8, jnp.logical_and(row >= 32, row < 40))
        start = jnp.where(diagonal, TAU_STAB, 0.0)
        sums = lax.fori_loop(0, MODES, body, start, unroll=8)
        at = pl.ds(j * LANES, LANES)
        parts_a[:, at] = jnp.concatenate(split3(sums[0:LANES]), axis=0)
        pay_b[pl.ds(0, 8), at] = sums[LANES:TRI]


def condense_loads(weighted_ref, coupling_ref, face_ref, pay_b):
    for j in range(EFACES):

        def body(k, sums):
            c = coupling_ref[k, j * FNODES : (j + 1) * FNODES, :].astype(F32)
            return tuple(
                sums[comp] + c * weighted_ref[comp, pl.ds(k, 1), :] for comp in range(COMPS)
            )

        start = (jnp.zeros((FNODES, LANES), F32),) * COMPS
        sums = lax.fori_loop(0, MODES, body, start, unroll=8)
        at = pl.ds(j * LANES, LANES)
        for comp in range(COMPS):
            pay_b[pl.ds(8 + comp * FNODES, FNODES), at] = (
                face_ref[comp, j * FNODES : (j + 1) * FNODES, :] - sums[comp]
            )
        pay_b[pl.ds(88, LANES - 88), at] = jnp.zeros((LANES - 88, LANES), F32)


def pick(hot, parts):
    found = dot(hot, parts, NT)
    return found[:, 0:LANES] + found[:, LANES : 2 * LANES] + found[:, 2 * LANES :]


def pack_rest(rows, z, out_ref, q):
    lane = iota((8, LANES), 1)
    sub = iota((8, LANES), 0)
    rest = rows[pl.ds(z, CAP, stride=16), :]
    x0, x1, x2 = rest[0:8], rest[8:16], rest[16:24]
    out_ref[q, 0:8, :] = jnp.where(lane < 64, x0, pltpu.roll(x1, 64, 1))
    out_ref[q, 8:16, :] = jnp.where(
        lane < 64,
        x2,
        jnp.where(
            lane < 88, x0, jnp.where(lane < 112, pltpu.roll(x1, 24, 1), pltpu.roll(x2, 48, 1))
        ),
    )
    spread = pltpu.roll(x2, 48, 1, stride=8, stride_axis=0)
    out_ref[q, 16:17, :] = jnp.sum(
        jnp.where((lane >> 3) == sub, spread, 0.0), axis=0, keepdims=True
    )


def unpack_rest(arrived_ref, p, rows, z):
    lane = iota((8, LANES), 1)
    sub = iota((8, LANES), 0)
    b = arrived_ref[p, 0:8, :]
    c = arrived_ref[p, 8:16, :]
    tail = jnp.broadcast_to(arrived_ref[p, 16:17, :], (8, LANES))
    spread = jnp.take_along_axis(pltpu.roll(tail, 24, 1, stride=8, stride_axis=0), 7 - sub, axis=0)
    zero = jnp.zeros((8, LANES), F32)
    base = pl.multiple_of(z * CAP, 8)
    rows[pl.ds(base, 8), :] = jnp.where(lane < 64, b, jnp.where(lane < 88, c, zero))
    rows[pl.ds(base + 8, 8), :] = jnp.where(
        lane < 64, pltpu.roll(b, 64, 1), jnp.where(lane < 88, pltpu.roll(c, 104, 1), zero)
    )
    rows[pl.ds(base + 16, 8), :] = jnp.where(
        lane < 64,
        c,
        jnp.where(lane < 80, pltpu.roll(c, 80, 1), jnp.where(lane < 88, spread, zero)),
    )


def pack_traces(rows, z, ret_ref, p):
    lane = iota((8, LANES), 1)
    base = pl.multiple_of(z * CAP, 8)
    y0 = rows[pl.ds(base, 8), :]
    y1 = rows[pl.ds(base + 8, 8), :]
    y2 = rows[pl.ds(base + 16, 8), :]
    ret_ref[p, 0:8, :] = jnp.where(lane < 64, y0, pltpu.roll(y1, 64, 1))
    second = jnp.where(
        lane < 64,
        y2,
        jnp.where(lane < 80, y0, jnp.where(lane < 96, pltpu.roll(y1, 16, 1), pltpu.roll(y2, 32, 1))),
    )
    last = jnp.broadcast_to(pltpu.roll(second, 16, 1)[7:8], (8, LANES))
    last = pltpu.roll(last, 0, 1, stride=16, stride_axis=0)
    ret_ref[p, 8:15, :] = jnp.where(lane < 112, second, last)[0:7]


def unpack_traces(back_ref, q, rows, z):
    lane = iota((8, LANES), 1)
    sub = iota((8, LANES), 0)
    zero = jnp.zeros((8, LANES), F32)
    b = back_ref[q, 0:8, :]
    c = jnp.concatenate([back_ref[q, 8:15, :], zero[0:1]], axis=0)
    last = pltpu.roll(jnp.take_along_axis(c, 7 - sub, axis=0), 0, 1, stride=16, stride_axis=0)
    last = jnp.sum(jnp.where((lane >> 4) == sub - 1, last, 0.0), axis=0, keepdims=True)
    c = jnp.where(sub < 7, c, jnp.broadcast_to(last, (8, LANES)))
    y0 = jnp.where(lane < 64, b, jnp.where(lane < 80, c, zero))
    y1 = jnp.where(
        lane < 64, pltpu.roll(b, 64, 1), jnp.where(lane < 80, pltpu.roll(c, 112, 1), zero)
    )
    y2 = jnp.where(lane < 64, c, jnp.where(lane < 80, pltpu.roll(c, 96, 1), zero))
    rows[pl.ds(z, CAP, stride=16), :] = jnp.concatenate([y0, y1, y2], axis=0)


def solve_faces(grid, idle):
    scaled = []
    lower = []
    inverse = []
    for j in range(FNODES):
        column = jnp.stack([grid[block_row(i, j)] for i in range(j, FNODES)], axis=0)
        for k in range(j):
            column = column - scaled[k][j - k :] * lower[k][j - k][None]
        pivot = 1.0 / (column[0] + idle)
        inverse.append(pivot)
        scaled.append(column)
        lower.append(column * pivot[None])
    forward = []
    for i in range(FNODES):
        total = jnp.stack([grid[TRI + comp * FNODES + i] for comp in range(COMPS)], axis=0)
        for k in range(i):
            total = total - lower[k][i - k][None] * forward[k]
        forward.append(total)
    solved = [None] * FNODES
    for i in reversed(range(FNODES)):
        total = forward[i] * inverse[i][None]
        for k in range(i + 1, FNODES):
            total = total - lower[i][k - i][None] * solved[k]
        solved[i] = total
    return solved


def ring_offset(n):
    t = N_Z - 1 - n
    half = lax.div(t + 1, 2)
    return lax.rem(16 + half * (2 * lax.rem(t, 2) - 1), 16)


def spread_slots(lists, slots):
    lane = iota((4, LANES), 1)
    rows = [lists[pl.ds(a, 4, stride=3), :] for a in range(3)]
    for z in range(N_Z):
        a, b = divmod(z * CAP, LANES)
        value = pltpu.roll(rows[a], LANES - b, 1) if b else rows[a]
        if b + CAP > LANES:
            value = jnp.where(lane < LANES - b, value, pltpu.roll(rows[a + 1], LANES - b, 1))
        slots[pl.ds(z, 4, stride=N_Z), :] = jnp.where(lane < CAP, value, SLOTS)


def step_kernel(
    density_hbm,
    speed_hbm,
    flags_hbm,
    mass_hbm,
    eigs_hbm,
    send_hbm,
    face_hbm,
    coupling_hbm,
    inner_hbm,
    faceres_hbm,
    traces_ref,
    coef_ref,
    density,
    speed_ref,
    flags,
    mass,
    eigs_ref,
    lists,
    face_ref,
    coupling,
    inner,
    faceres,
    slots_ref,
    weighted,
    eps_out,
    eps_in,
    visc_out,
    visc_in,
    top_out,
    tops,
    slot_hot,
    row_hot,
    products,
    masks,
    pay_b,
    parts_a,
    parts_b,
    rows,
    whole_out,
    whole_in,
    rest_out,
    rest_in,
    joined_a,
    joined_b,
    grid,
    answer,
    returning,
    back,
    load_sem,
    send_a,
    recv_a,
    send_b,
    recv_b,
    send_c,
    recv_c,
    send_d,
    recv_d,
    send_e,
    recv_e,
    send_f,
    recv_f,
):
    me = lax.axis_index("dom")
    group = lax.axis_index("group")
    my_y = lax.div(me, N_Z)
    my_z = lax.rem(me, N_Z)
    following = {"dom": lax.rem(me + 1, N_DOM)}
    barrier = pltpu.get_barrier_semaphore()

    def each_peer(act):
        def one_z(n, carry):
            z = lax.rem(my_z + ring_offset(n), N_Z)
            for dy in (2, 1, 3, 0):
                act(lax.rem(my_y + dy, N_Y) * N_Z + z)
            return carry

        lax.fori_loop(0, N_Z - 1, one_z, 0)
        for dy in (2, 1, 3):
            act(lax.rem(my_y + dy, N_Y) * N_Z + my_z)

    def each_group(act):
        def one(k, carry):
            act(lax.rem(group + k, N_GROUP))
            return carry

        lax.fori_loop(1, N_GROUP, one, 0)

    each_peer(
        lambda q: pl.semaphore_signal(barrier, inc=1, device_id={"dom": q}, device_id_type=MESH)
    )
    each_group(
        lambda g: pl.semaphore_signal(barrier, inc=1, device_id={"group": g}, device_id_type=MESH)
    )
    loads = [
        pltpu.make_async_copy(source, target, load_sem.at[n])
        for n, (source, target) in enumerate(
            (
                (density_hbm, density),
                (speed_hbm, speed_ref),
                (flags_hbm, flags),
                (send_hbm, lists),
                (face_hbm, face_ref),
                (coupling_hbm, coupling),
                (mass_hbm, mass),
                (eigs_hbm, eigs_ref),
                (inner_hbm, inner),
                (faceres_hbm, faceres),
            )
        )
    ]
    for copy in loads:
        copy.start()
    for copy in loads[:5]:
        copy.wait()

    speed = speed_ref[...]
    eps = element_eps(density[...], speed, flags[...])
    spread_slots(lists, slots_ref)
    slots = slots_ref[...]
    lane = iota((N_DOM, LANES), 1)
    values = jnp.take_along_axis(
        jnp.broadcast_to(eps, (N_DOM, LANES)), slots & (ELEM_DEV - 1), axis=1
    )
    values = jnp.where(slots < SLOTS, values, 0.0)
    values = jnp.where(lane == LANES - 1, jnp.max(speed, axis=1, keepdims=True), values)
    for q in range(N_DOM):
        eps_out[q] = values[q : q + 1, :]

    for y in range(N_Y):
        for i in range(CAP):
            column = slots[y * N_Z : (y + 1) * N_Z, i : i + 1]
            slot_hot[y, i * N_Z : (i + 1) * N_Z, :] = one_hot(iota((N_Z, SLOTS), 1) == column)

    pl.semaphore_wait(barrier, N_DOM + N_GROUP - 2)
    each_peer(
        lambda q: remote(eps_out.at[q], eps_in.at[me], send_a, recv_a, {"dom": q}).start()
    )
    eps_in[me] = eps_out[me]
    partner_p, partner_i = partner_rows(face_ref)
    loads[5].wait()
    multiply_blocks(coupling, products)
    others = pl.ds(0, N_DOM - 1)
    first_leg = remote(eps_out.at[others], eps_in.at[others], send_a, recv_a, following)
    first_leg.wait_recv()

    partner_eps = jnp.zeros((16, LANES), F32)
    top = jnp.zeros((1, LANES), F32)
    for p in range(N_DOM):
        row = eps_in[p]
        top = jnp.maximum(top, row)
        found = jnp.take_along_axis(jnp.broadcast_to(row, (16, LANES)), partner_i, axis=1)
        partner_eps = jnp.where(partner_p == p, found, partner_eps)
    for r in range(16):
        visc_out[r] = partner_eps[r : r + 1, :]
    top_out[0] = top
    each_peer(
        lambda p: remote(
            visc_out.at[lax.div(p, 4)], visc_in.at[me], send_b, recv_b, {"dom": p}
        ).start()
    )
    each_group(
        lambda g: remote(top_out.at[0], tops.at[group], send_c, recv_c, {"group": g}).start()
    )
    visc_in[me] = visc_out[lax.div(me, 4)]
    tops[group] = top_out[0]

    for y in range(N_Y):
        received = iota((PART, FACES), 0) + y * PART
        row_hot[y] = one_hot(
            jnp.logical_or(received == face_ref[0:1, :], received == face_ref[1:2, :])
        )
    for i in range(CAP):
        slot = slots[:, i : i + 1]
        here = jnp.logical_and((slot & (ELEM_DEV - 1)) == lane, slot < SLOTS)
        masks[i] = jnp.where(here, 1.0, 0.0)
    for copy in loads[6:]:
        copy.wait()

    second_leg = remote(eps_in.at[others], visc_in.at[others], send_b, recv_b, following)
    second_leg.wait_recv()
    seven = pl.ds(0, N_GROUP - 1)
    top_leg = remote(
        tops.at[seven],
        tops.at[seven],
        send_c,
        recv_c,
        {"group": lax.rem(group + 1, N_GROUP)},
    )
    top_leg.wait_recv()

    came = jnp.concatenate([visc_in[q] for q in range(N_DOM)], axis=0)
    came = pltpu.roll(came, lax.rem(4 - lax.rem(me, 4), 4) * 32, 1)
    total = jnp.zeros((N_DOM, LANES), F32)
    for i in range(CAP):
        total = total + masks[i] * came[:, i : i + 1]
    gathered = jnp.sum(total, axis=0, keepdims=True)
    nu = NU_BASE + (EFACES * eps + gathered) / (2.0 * EFACES)
    top = tops[0]
    for g in range(1, N_GROUP):
        top = jnp.maximum(top, tops[g])
    peak = jnp.max(jnp.where(iota((1, LANES), 1) == LANES - 1, top, 0.0), axis=1, keepdims=True)
    square = iota((MODES, MODES), 0) == iota((MODES, MODES), 1)
    eigs = jnp.sum(jnp.where(square, eigs_ref[...], 0.0), axis=1, keepdims=True)
    coef = 1.0 / (mass[...] * (1.0 + speed / peak + nu * eigs))
    coef_ref[...] = coef

    condense_blocks(coef_ref, products, parts_a, pay_b)
    for c in range(N_Y):
        y = lax.rem(my_y + c, N_Y)
        rows[...] = pick(slot_hot[y], parts_a[...])

        def send_whole(n, carry):
            z = lax.rem(my_z + ring_offset(n), N_Z)
            q = y * N_Z + z
            whole_out[q] = rows[pl.ds(z, CAP, stride=16), :]
            remote(whole_out.at[q], whole_in.at[me], send_d, recv_d.at[c], {"dom": q}).start()
            return carry

        lax.fori_loop(0, N_Z if c else N_Z - 1, send_whole, 0)
        if c == 0:
            whole_in[me] = rows[pl.ds(my_z, CAP, stride=16), :]
    weighted[...] = inner[...] * coef[None]
    condense_loads(weighted, coupling, faceres, pay_b)
    parts_b[...] = jnp.concatenate(split3(pay_b[...]), axis=0)
    for c in range(N_Y):
        y = lax.rem(my_y + c, N_Y)
        rows[...] = pick(slot_hot[y], parts_b[...])

        def send_rest(n, carry):
            z = lax.rem(my_z + ring_offset(n), N_Z)
            q = y * N_Z + z
            pack_rest(rows, z, rest_out, q)
            remote(rest_out.at[q], rest_in.at[me], send_e, recv_e.at[c], {"dom": q}).start()
            return carry

        lax.fori_loop(0, N_Z if c else N_Z - 1, send_rest, 0)
        if c == 0:
            pack_rest(rows, my_z, rest_in, me)

    def to_grid(joined, start, height):
        for chunk in range(6):
            for n in range(height // 8):
                grid[start + n * 8 : start + n * 8 + 8, chunk, :] = joined[
                    n * 8 : n * 8 + 8, chunk * LANES : (chunk + 1) * LANES
                ]

    for c in range(N_Y):
        y = lax.rem(my_y + N_Y - c, N_Y)
        sources = pl.ds(0, N_Z if c else N_Z - 1)
        remote(
            whole_out.at[sources], whole_in.at[sources], send_d, recv_d.at[c], following
        ).wait_recv()
        came = whole_in[pl.ds(pl.multiple_of(y * N_Z, N_Z), N_Z)].reshape(PART, LANES)
        stacked = jnp.concatenate(split3(jnp.transpose(came)), axis=0)
        found = dot(stacked, row_hot[y], NN)
        found = found[0:LANES] + found[LANES : 2 * LANES] + found[2 * LANES :]
        joined_a[...] = found if c == 0 else joined_a[...] + found
    to_grid(joined_a, 0, LANES)
    for c in range(N_Y):
        y = lax.rem(my_y + N_Y - c, N_Y)
        sources = pl.ds(0, N_Z if c else N_Z - 1)
        remote(
            rest_out.at[sources], rest_in.at[sources], send_e, recv_e.at[c], following
        ).wait_recv()

        def take_rest(z, carry):
            unpack_rest(rest_in, y * N_Z + z, rows, z)
            return carry

        lax.fori_loop(0, N_Z, take_rest, 0, unroll=2)
        stacked = jnp.concatenate(split3(jnp.transpose(rows[...])[0:HALF]), axis=0)
        found = dot(stacked, row_hot[y], NN)
        found = found[0:HALF] + found[HALF : 2 * HALF] + found[2 * HALF :]
        joined_b[...] = found if c == 0 else joined_b[...] + found
    to_grid(joined_b, LANES, USED - LANES)
    first = face_ref[0:1, :]
    idle = jnp.concatenate(
        [first[:, chunk * LANES : (chunk + 1) * LANES] for chunk in range(6)]
        + [jnp.full((2, LANES), ROWS, I32)],
        axis=0,
    )
    idle = jnp.where(idle < ROWS, 0.0, 1.0)
    solved = solve_faces(grid, idle)
    for i in range(FNODES):
        for comp in range(COMPS):
            answer[comp * FNODES + i] = solved[i][comp]
    face_traces = jnp.concatenate([answer[:, chunk, :] for chunk in range(6)], axis=1)
    gap = jnp.zeros((LANES - COMPS * FNODES, FACES), BF16)
    high, low = split2(face_traces)
    both = jnp.concatenate([high, gap, low, gap], axis=0)

    for c in range(N_Y):
        y = lax.rem(my_y + c, N_Y)
        found = dot(row_hot[y], both, NT)
        rows[...] = found[:, 0:LANES] + found[:, LANES : 2 * LANES]

        def send_traces(n, carry):
            z = lax.rem(my_z + ring_offset(n), N_Z)
            p = y * N_Z + z
            pack_traces(rows, z, returning, p)
            remote(returning.at[p], back.at[me], send_f, recv_f.at[c], {"dom": p}).start()
            return carry

        lax.fori_loop(0, N_Z if c else N_Z - 1, send_traces, 0)
        if c == 0:
            pack_traces(rows, my_z, back, me)

    for c in range(N_Y):
        y = lax.rem(my_y + N_Y - c, N_Y)
        sources = pl.ds(0, N_Z if c else N_Z - 1)
        remote(returning.at[sources], back.at[sources], send_f, recv_f.at[c], following).wait_recv()

        def take_traces(z, carry):
            unpack_traces(back, y * N_Z + z, rows, z)
            return carry

        lax.fori_loop(0, N_Z, take_traces, 0, unroll=2)
        turned = jnp.transpose(rows[...])[0 : COMPS * FNODES]
        stacked = jnp.concatenate(split2(turned), axis=0)
        found = dot(stacked, slot_hot[y], NN)
        found = found[0 : COMPS * FNODES] + found[COMPS * FNODES :]
        for comp in range(COMPS):
            for j in range(EFACES):
                piece = found[comp * FNODES : (comp + 1) * FNODES, j * LANES : (j + 1) * LANES]
                at = slice(j * FNODES, (j + 1) * FNODES)
                traces_ref[comp, at, :] = piece if c == 0 else traces_ref[comp, at, :] + piece
    remote(rest_out.at[others], rest_in.at[others], send_e, recv_e.at[0], following).wait_send()
    remote(returning.at[others], back.at[others], send_f, recv_f.at[0], following).wait_send()
    for leg in (first_leg, second_leg, top_leg):
        leg.wait_send()
    remote(whole_out.at[others], whole_in.at[others], send_d, recv_d.at[0], following).wait_send()


def update_kernel(traces_in, coef_ref, coupling_ref, inner_ref, update_ref, traces_ref):
    traces_ref[...] = traces_in[...]

    def substitute(k, carry):
        c = coupling_ref[k].astype(F32)
        coef = coef_ref[pl.ds(k, 1), :]
        for comp in range(COMPS):
            pulled = jnp.sum(c * traces_in[comp], axis=0, keepdims=True)
            update_ref[comp, pl.ds(k, 1), :] = coef * (inner_ref[comp, pl.ds(k, 1), :] - pulled)
        return carry

    lax.fori_loop(0, MODES, substitute, 0, unroll=4)


def local(
    density_modes,
    wave_speed,
    shock_flags,
    elem_mass,
    stiff_eigs,
    coupling,
    interior_res,
    face_res,
    send_rows,
    face_rows,
):
    vmem = pl.BlockSpec(memory_space=pltpu.VMEM)
    anywhere = pl.BlockSpec(memory_space=pltpu.HBM)
    dma = pltpu.SemaphoreType.DMA
    traces, coef = pl.pallas_call(
        step_kernel,
        out_shape=(
            pltpu.VMEM((COMPS, TRACE, LANES), F32),
            pltpu.VMEM((MODES, LANES), F32),
        ),
        in_specs=[anywhere] * 10,
        out_specs=(vmem, vmem),
        scratch_shapes=[
            pltpu.VMEM((MODES, LANES), F32),
            pltpu.VMEM((1, LANES), F32),
            pltpu.VMEM((1, LANES), I32),
            pltpu.VMEM((1, LANES), F32),
            pltpu.VMEM((1, MODES), F32),
            pltpu.VMEM((12, LANES), I32),
            pltpu.VMEM((2, FACES), I32),
            pltpu.VMEM((MODES, TRACE, LANES), BF16),
            pltpu.VMEM((COMPS, MODES, LANES), F32),
            pltpu.VMEM((COMPS, TRACE, LANES), F32),
            pltpu.VMEM((N_DOM, LANES), I32),
            pltpu.VMEM((COMPS, MODES, LANES), F32),
            pltpu.VMEM((N_DOM, 1, LANES), F32),
            pltpu.VMEM((N_DOM, 1, LANES), F32),
            pltpu.VMEM((16, 1, LANES), F32),
            pltpu.VMEM((N_DOM, 1, LANES), F32),
            pltpu.VMEM((1, 1, LANES), F32),
            pltpu.VMEM((N_GROUP, 1, LANES), F32),
            pltpu.VMEM((N_Y, PART, SLOTS), BF16),
            pltpu.VMEM((N_Y, PART, FACES), BF16),
            pltpu.VMEM((EFACES, MODES, TRI, LANES), F32),
            pltpu.VMEM((CAP, N_DOM, LANES), F32),
            pltpu.VMEM((LANES, SLOTS), F32),
            pltpu.VMEM((3 * LANES, SLOTS), BF16),
            pltpu.VMEM((3 * LANES, SLOTS), BF16),
            pltpu.VMEM((PART, LANES), F32),
            pltpu.VMEM((N_DOM, CAP, LANES), F32),
            pltpu.VMEM((N_DOM, CAP, LANES), F32),
            pltpu.VMEM((N_DOM, REST_TILE, LANES), F32),
            pltpu.VMEM((N_DOM, REST_TILE, LANES), F32),
            pltpu.VMEM((LANES, FACES), F32),
            pltpu.VMEM((HALF, FACES), F32),
            pltpu.VMEM((USED, 8, LANES), F32),
            pltpu.VMEM((COMPS * FNODES, 8, LANES), F32),
            pltpu.VMEM((N_DOM, RET_TILE, LANES), F32),
            pltpu.VMEM((N_DOM, RET_TILE, LANES), F32),
            dma((10,)),
            dma,
            dma,
            dma,
            dma,
            dma,
            dma,
            dma,
            dma((N_Y,)),
            dma,
            dma((N_Y,)),
            dma,
            dma((N_Y,)),
        ],
        compiler_params=pltpu.CompilerParams(
            collective_id=0, has_side_effects=True, vmem_limit_bytes=VMEM_LIMIT
        ),
        name="newton_step",
    )(
        density_modes,
        wave_speed[None, :],
        shock_flags[None, :],
        elem_mass[None, :],
        stiff_eigs[None, :],
        send_rows.reshape(12, LANES),
        face_rows,
        coupling,
        interior_res,
        face_res,
    )
    return pl.pallas_call(
        update_kernel,
        out_shape=(
            jax.ShapeDtypeStruct((COMPS, MODES, LANES), F32),
            jax.ShapeDtypeStruct((COMPS, TRACE, LANES), F32),
        ),
        in_specs=[vmem] * 4,
        out_specs=(vmem, vmem),
        compiler_params=pltpu.CompilerParams(vmem_limit_bytes=16 * 1024 * 1024),
        name="back_substitute",
    )(traces, coef, coupling, interior_res)


def solution(mesh):
    return jax.shard_map(
        local,
        mesh=mesh,
        in_specs=(
            P(None, ("group", "dom")),
            P(("group", "dom")),
            P(("group", "dom")),
            P(("group", "dom")),
            P(),
            P(None, None, ("group", "dom")),
            P(None, None, ("group", "dom")),
            P(None, None, ("group", "dom")),
            P(("group", "dom")),
            P(None, ("group", "dom")),
        ),
        out_specs=(P(None, None, ("group", "dom")), P(None, None, ("group", "dom"))),
        check_vma=False,
    )
```

```python
import jax
import jax.numpy as jnp
from jax import lax
from jax.experimental import pallas as pl
from jax.experimental.pallas import tpu as pltpu
from jax.sharding import PartitionSpec as P

MODES = 64
FNODES = 16
COMPS = 5
EFACES = 6
TRACE = 96
ELEM_DEV = 128
SLOTS = EFACES * ELEM_DEV
CAP = 24
N_DOM = 64
N_GROUP = 8
ROWS = N_DOM * CAP
FACES = 768
TRI = 136
USED = 216
N_Z = 16
N_Y = N_DOM // N_Z
Y_ORDER = (2, 1, 3, 0)
PART = N_Z * CAP
LANES = 128
HALF = 96
REST_TILE = 17
RET_TILE = 15

EPS_SCALE = 0.1
NU_BASE = 0.02
TAU_STAB = 1.0
SENSOR_MID = -2.0
SENSOR_WIDTH = 0.5
RATIO_FLOOR = 0.0001

F32 = jnp.float32
BF16 = jnp.bfloat16
I32 = jnp.int32
MESH = pl.DeviceIdType.MESH
NN = (((1,), (0,)), ((), ()))
NT = (((1,), (1,)), ((), ()))
VMEM_LIMIT = 60 * 1024 * 1024


def iota(shape, axis):
    return lax.broadcasted_iota(I32, shape, axis)


def split3(x):
    high = x.astype(BF16)
    rest = x - high.astype(F32)
    middle = rest.astype(BF16)
    low = (rest - middle.astype(F32)).astype(BF16)
    return high, middle, low


def split2(x):
    high = x.astype(BF16)
    return high, (x - high.astype(F32)).astype(BF16)


def dot(a, b, dims):
    return lax.dot_general(a, b, dims, preferred_element_type=F32)


def one_hot(mask):
    return jnp.where(mask, 1.0, 0.0).astype(BF16)


def element_eps(density, speed, flags):
    ids = iota((MODES, LANES), 0)
    degree = jnp.maximum(jnp.maximum(ids >> 4, (ids >> 2) & 3), ids & 3)
    squares = density * density
    totals = jnp.sum(squares, axis=0, keepdims=True) + 1e-06
    high = jnp.sum(jnp.where(degree == 3, squares, 0.0), axis=0, keepdims=True)
    sensor = jnp.log10(jnp.maximum(high / totals, RATIO_FLOOR))
    ramped = 0.5 * (1.0 + jnp.tanh((sensor - SENSOR_MID) / SENSOR_WIDTH))
    return EPS_SCALE * speed * jnp.maximum(ramped, 0.5 * flags.astype(F32))


def padded_row(row):
    source = (row * 2731) >> 16
    return source, row - source * CAP


def partner_rows(face_ref):
    pieces = [
        face_ref[end : end + 1, chunk * LANES : (chunk + 1) * LANES]
        for end in range(2)
        for chunk in range(6)
    ]
    stacked = jnp.concatenate(pieces + [jnp.zeros((LANES - 12, LANES), I32)], axis=0)
    turned = jnp.transpose(stacked.astype(F32)).astype(I32)
    high_parts = []
    low_parts = []
    for end in range(2):
        own_p, own_i = padded_row(face_ref[end : end + 1, :])
        other_p, other_i = padded_row(face_ref[1 - end : 2 - end, :])
        mine = iota((16, FACES), 0) == (own_p >> 2)
        high_parts.append(
            jnp.concatenate(
                [
                    jnp.where(mine, other_p.astype(F32), 0.0),
                    jnp.where(mine, other_i.astype(F32), 0.0),
                ],
                axis=0,
            ).astype(BF16)
        )
        columns = []
        for chunk in range(6):
            n = end * 6 + chunk
            col_p, col_i = padded_row(turned[:, n : n + 1])
            place = ((col_p & 3) << 5) + col_i
            columns.append(one_hot(iota((LANES, LANES), 1) == place))
        low_parts.append(jnp.concatenate(columns, axis=0))
    found = dot(high_parts[0], low_parts[0], NN) + dot(high_parts[1], low_parts[1], NN)
    found = found.astype(I32)
    return found[0:16], found[16:32]


def remote(src, dst, send_sem, recv_sem, where):
    return pltpu.make_async_remote_copy(
        src_ref=src,
        dst_ref=dst,
        send_sem=send_sem,
        recv_sem=recv_sem,
        device_id=where,
        device_id_type=MESH,
    )


def block_row(i, j):
    d = (i - j) % 8
    if i >= 8 > j:
        return 64 + d * 8 + j
    base = 32 if j >= 8 else 0
    low, high = j % 8, i % 8
    if d < 4:
        return base + d * 8 + low
    if d > 4:
        return base + (8 - d) * 8 + high
    return 128 + (high if base else low)


def multiply_blocks(coupling_ref, products):
    sub = iota((8, LANES), 0)

    def body(k, carry):
        for j in range(EFACES):
            c = coupling_ref[k, j * FNODES : (j + 1) * FNODES, :].astype(F32)
            c0, c1 = c[0:8], c[8:16]
            turned = [c1] + [pltpu.roll(c1, 8 - d, 0) for d in range(1, 8)]
            for d in range(4):
                products[j, k, d * 8 : d * 8 + 8, :] = c0 * (pltpu.roll(c0, 8 - d, 0) if d else c0)
                products[j, k, 32 + d * 8 : 40 + d * 8, :] = c1 * turned[d]
            for d in range(8):
                products[j, k, 64 + d * 8 : 72 + d * 8, :] = c0 * turned[d]
            products[j, k, 128:136, :] = jnp.where(
                sub < 4, c0 * pltpu.roll(c0, 4, 0), c1 * turned[4]
            )
        return carry

    lax.fori_loop(0, MODES, body, 0)


def condense_blocks(coef_ref, products, parts_a, pay_b):
    for j in range(EFACES):

        def body(k, sums):
            return sums + coef_ref[pl.ds(k, 1), :] * products[j, k]

        row = iota((TRI, LANES), 0)
        diagonal = jnp.logical_or(row < 8, jnp.logical_and(row >= 32, row < 40))
        start = jnp.where(diagonal, TAU_STAB, 0.0)
        sums = lax.fori_loop(0, MODES, body, start, unroll=8)
        at = pl.ds(j * LANES, LANES)
        parts_a[:, at] = jnp.concatenate(split3(sums[0:LANES]), axis=0)
        pay_b[pl.ds(0, 8), at] = sums[LANES:TRI]


def condense_loads(weighted_ref, coupling_ref, face_ref, pay_b):
    for j in range(EFACES):

        def body(k, sums):
            c = coupling_ref[k, j * FNODES : (j + 1) * FNODES, :].astype(F32)
            return tuple(
                sums[comp] + c * weighted_ref[comp, pl.ds(k, 1), :] for comp in range(COMPS)
            )

        start = (jnp.zeros((FNODES, LANES), F32),) * COMPS
        sums = lax.fori_loop(0, MODES, body, start, unroll=8)
        at = pl.ds(j * LANES, LANES)
        for comp in range(COMPS):
            pay_b[pl.ds(8 + comp * FNODES, FNODES), at] = (
                face_ref[comp, j * FNODES : (j + 1) * FNODES, :] - sums[comp]
            )
        pay_b[pl.ds(88, LANES - 88), at] = jnp.zeros((LANES - 88, LANES), F32)


def pick(hot, parts):
    found = dot(hot, parts, NT)
    return found[:, 0:LANES] + found[:, LANES : 2 * LANES] + found[:, 2 * LANES :]


def pack_rest(rows, z, out_ref, q):
    lane = iota((8, LANES), 1)
    sub = iota((8, LANES), 0)
    rest = rows[pl.ds(z, CAP, stride=16), :]
    x0, x1, x2 = rest[0:8], rest[8:16], rest[16:24]
    out_ref[q, 0:8, :] = jnp.where(lane < 64, x0, pltpu.roll(x1, 64, 1))
    out_ref[q, 8:16, :] = jnp.where(
        lane < 64,
        x2,
        jnp.where(
            lane < 88, x0, jnp.where(lane < 112, pltpu.roll(x1, 24, 1), pltpu.roll(x2, 48, 1))
        ),
    )
    spread = pltpu.roll(x2, 48, 1, stride=8, stride_axis=0)
    out_ref[q, 16:17, :] = jnp.sum(
        jnp.where((lane >> 3) == sub, spread, 0.0), axis=0, keepdims=True
    )


def unpack_rest(arrived_ref, p, rows, z):
    lane = iota((8, LANES), 1)
    sub = iota((8, LANES), 0)
    b = arrived_ref[p, 0:8, :]
    c = arrived_ref[p, 8:16, :]
    tail = jnp.broadcast_to(arrived_ref[p, 16:17, :], (8, LANES))
    spread = jnp.take_along_axis(pltpu.roll(tail, 24, 1, stride=8, stride_axis=0), 7 - sub, axis=0)
    zero = jnp.zeros((8, LANES), F32)
    base = pl.multiple_of(z * CAP, 8)
    rows[pl.ds(base, 8), :] = jnp.where(lane < 64, b, jnp.where(lane < 88, c, zero))
    rows[pl.ds(base + 8, 8), :] = jnp.where(
        lane < 64, pltpu.roll(b, 64, 1), jnp.where(lane < 88, pltpu.roll(c, 104, 1), zero)
    )
    rows[pl.ds(base + 16, 8), :] = jnp.where(
        lane < 64,
        c,
        jnp.where(lane < 80, pltpu.roll(c, 80, 1), jnp.where(lane < 88, spread, zero)),
    )


def pack_traces(rows, z, ret_ref, p):
    lane = iota((8, LANES), 1)
    base = pl.multiple_of(z * CAP, 8)
    y0 = rows[pl.ds(base, 8), :]
    y1 = rows[pl.ds(base + 8, 8), :]
    y2 = rows[pl.ds(base + 16, 8), :]
    ret_ref[p, 0:8, :] = jnp.where(lane < 64, y0, pltpu.roll(y1, 64, 1))
    second = jnp.where(
        lane < 64,
        y2,
        jnp.where(lane < 80, y0, jnp.where(lane < 96, pltpu.roll(y1, 16, 1), pltpu.roll(y2, 32, 1))),
    )
    last = jnp.broadcast_to(pltpu.roll(second, 16, 1)[7:8], (8, LANES))
    last = pltpu.roll(last, 0, 1, stride=16, stride_axis=0)
    ret_ref[p, 8:15, :] = jnp.where(lane < 112, second, last)[0:7]


def unpack_traces(back_ref, q, rows, z):
    lane = iota((8, LANES), 1)
    sub = iota((8, LANES), 0)
    zero = jnp.zeros((8, LANES), F32)
    b = back_ref[q, 0:8, :]
    c = jnp.concatenate([back_ref[q, 8:15, :], zero[0:1]], axis=0)
    last = pltpu.roll(jnp.take_along_axis(c, 7 - sub, axis=0), 0, 1, stride=16, stride_axis=0)
    last = jnp.sum(jnp.where((lane >> 4) == sub - 1, last, 0.0), axis=0, keepdims=True)
    c = jnp.where(sub < 7, c, jnp.broadcast_to(last, (8, LANES)))
    y0 = jnp.where(lane < 64, b, jnp.where(lane < 80, c, zero))
    y1 = jnp.where(
        lane < 64, pltpu.roll(b, 64, 1), jnp.where(lane < 80, pltpu.roll(c, 112, 1), zero)
    )
    y2 = jnp.where(lane < 64, c, jnp.where(lane < 80, pltpu.roll(c, 96, 1), zero))
    rows[pl.ds(z, CAP, stride=16), :] = jnp.concatenate([y0, y1, y2], axis=0)


def solve_faces(grid, idle):
    scaled = []
    lower = []
    inverse = []
    for j in range(FNODES):
        column = jnp.stack([grid[block_row(i, j)] for i in range(j, FNODES)], axis=0)
        for k in range(j):
            column = column - scaled[k][j - k :] * lower[k][j - k][None]
        pivot = 1.0 / (column[0] + idle)
        inverse.append(pivot)
        scaled.append(column)
        lower.append(column * pivot[None])
    forward = []
    for i in range(FNODES):
        total = jnp.stack([grid[TRI + comp * FNODES + i] for comp in range(COMPS)], axis=0)
        for k in range(i):
            total = total - lower[k][i - k][None] * forward[k]
        forward.append(total)
    solved = [None] * FNODES
    for i in reversed(range(FNODES)):
        total = forward[i] * inverse[i][None]
        for k in range(i + 1, FNODES):
            total = total - lower[i][k - i][None] * solved[k]
        solved[i] = total
    return solved


def ring_offset(n):
    t = N_Z - 1 - n
    half = lax.div(t + 1, 2)
    return lax.rem(16 + half * (2 * lax.rem(t, 2) - 1), 16)


def spread_slots(lists, slots):
    lane = iota((4, LANES), 1)
    rows = [lists[pl.ds(a, 4, stride=3), :] for a in range(3)]
    for z in range(N_Z):
        a, b = divmod(z * CAP, LANES)
        value = pltpu.roll(rows[a], LANES - b, 1) if b else rows[a]
        if b + CAP > LANES:
            value = jnp.where(lane < LANES - b, value, pltpu.roll(rows[a + 1], LANES - b, 1))
        slots[pl.ds(z, 4, stride=N_Z), :] = jnp.where(lane < CAP, value, SLOTS)


def step_kernel(
    density_hbm,
    speed_hbm,
    flags_hbm,
    mass_hbm,
    eigs_hbm,
    send_hbm,
    face_hbm,
    coupling_hbm,
    inner_hbm,
    faceres_hbm,
    traces_ref,
    coef_ref,
    density,
    speed_ref,
    flags,
    mass,
    eigs_ref,
    lists,
    face_ref,
    coupling,
    inner,
    faceres,
    slots_ref,
    weighted,
    eps_out,
    eps_in,
    visc_out,
    visc_in,
    top_out,
    tops,
    slot_hot,
    row_hot,
    products,
    masks,
    pay_b,
    parts_a,
    parts_b,
    rows,
    whole_out,
    whole_in,
    rest_out,
    rest_in,
    joined_a,
    joined_b,
    grid,
    answer,
    returning,
    back,
    load_sem,
    send_a,
    recv_a,
    send_b,
    recv_b,
    send_c,
    recv_c,
    send_d,
    recv_d,
    send_e,
    recv_e,
    send_f,
    recv_f,
):
    me = lax.axis_index("dom")
    group = lax.axis_index("group")
    my_y = lax.div(me, N_Z)
    my_z = lax.rem(me, N_Z)
    following = {"dom": lax.rem(me + 1, N_DOM)}
    barrier = pltpu.get_barrier_semaphore()

    def each_peer(act):
        def one_z(n, carry):
            z = lax.rem(my_z + ring_offset(n), N_Z)
            for dy in (2, 1, 3, 0):
                act(lax.rem(my_y + dy, N_Y) * N_Z + z)
            return carry

        lax.fori_loop(0, N_Z - 1, one_z, 0)
        for dy in (2, 1, 3):
            act(lax.rem(my_y + dy, N_Y) * N_Z + my_z)

    def each_group(act):
        def one(k, carry):
            act(lax.rem(group + k, N_GROUP))
            return carry

        lax.fori_loop(1, N_GROUP, one, 0)

    each_peer(
        lambda q: pl.semaphore_signal(barrier, inc=1, device_id={"dom": q}, device_id_type=MESH)
    )
    each_group(
        lambda g: pl.semaphore_signal(barrier, inc=1, device_id={"group": g}, device_id_type=MESH)
    )
    loads = [
        pltpu.make_async_copy(source, target, load_sem.at[n])
        for n, (source, target) in enumerate(
            (
                (density_hbm, density),
                (speed_hbm, speed_ref),
                (flags_hbm, flags),
                (send_hbm, lists),
                (face_hbm, face_ref),
                (coupling_hbm, coupling),
                (mass_hbm, mass),
                (eigs_hbm, eigs_ref),
                (inner_hbm, inner),
                (faceres_hbm, faceres),
            )
        )
    ]
    for copy in loads:
        copy.start()
    for copy in loads[:5]:
        copy.wait()

    speed = speed_ref[...]
    eps = element_eps(density[...], speed, flags[...])
    spread_slots(lists, slots_ref)
    slots = slots_ref[...]
    lane = iota((N_DOM, LANES), 1)
    values = jnp.take_along_axis(
        jnp.broadcast_to(eps, (N_DOM, LANES)), slots & (ELEM_DEV - 1), axis=1
    )
    values = jnp.where(slots < SLOTS, values, 0.0)
    values = jnp.where(lane == LANES - 1, jnp.max(speed, axis=1, keepdims=True), values)
    for q in range(N_DOM):
        eps_out[q] = values[q : q + 1, :]

    for y in range(N_Y):
        for i in range(CAP):
            column = slots[y * N_Z : (y + 1) * N_Z, i : i + 1]
            slot_hot[y, i * N_Z : (i + 1) * N_Z, :] = one_hot(iota((N_Z, SLOTS), 1) == column)

    pl.semaphore_wait(barrier, N_DOM + N_GROUP - 2)
    each_peer(
        lambda q: remote(eps_out.at[q], eps_in.at[me], send_a, recv_a, {"dom": q}).start()
    )
    eps_in[me] = eps_out[me]
    partner_p, partner_i = partner_rows(face_ref)
    loads[5].wait()
    multiply_blocks(coupling, products)
    others = pl.ds(0, N_DOM - 1)
    first_leg = remote(eps_out.at[others], eps_in.at[others], send_a, recv_a, following)
    first_leg.wait_recv()

    partner_eps = jnp.zeros((16, LANES), F32)
    top = jnp.zeros((1, LANES), F32)
    for p in range(N_DOM):
        row = eps_in[p]
        top = jnp.maximum(top, row)
        found = jnp.take_along_axis(jnp.broadcast_to(row, (16, LANES)), partner_i, axis=1)
        partner_eps = jnp.where(partner_p == p, found, partner_eps)
    for r in range(16):
        visc_out[r] = partner_eps[r : r + 1, :]
    top_out[0] = top
    each_peer(
        lambda p: remote(
            visc_out.at[lax.div(p, 4)], visc_in.at[me], send_b, recv_b, {"dom": p}
        ).start()
    )
    each_group(
        lambda g: remote(top_out.at[0], tops.at[group], send_c, recv_c, {"group": g}).start()
    )
    visc_in[me] = visc_out[lax.div(me, 4)]
    tops[group] = top_out[0]

    for y in range(N_Y):
        received = iota((PART, FACES), 0) + y * PART
        row_hot[y] = one_hot(
            jnp.logical_or(received == face_ref[0:1, :], received == face_ref[1:2, :])
        )
    for i in range(CAP):
        slot = slots[:, i : i + 1]
        here = jnp.logical_and((slot & (ELEM_DEV - 1)) == lane, slot < SLOTS)
        masks[i] = jnp.where(here, 1.0, 0.0)
    for copy in loads[6:]:
        copy.wait()

    second_leg = remote(eps_in.at[others], visc_in.at[others], send_b, recv_b, following)
    second_leg.wait_recv()
    seven = pl.ds(0, N_GROUP - 1)
    top_leg = remote(
        tops.at[seven],
        tops.at[seven],
        send_c,
        recv_c,
        {"group": lax.rem(group + 1, N_GROUP)},
    )
    top_leg.wait_recv()

    came = jnp.concatenate([visc_in[q] for q in range(N_DOM)], axis=0)
    came = pltpu.roll(came, lax.rem(4 - lax.rem(me, 4), 4) * 32, 1)
    total = jnp.zeros((N_DOM, LANES), F32)
    for i in range(CAP):
        total = total + masks[i] * came[:, i : i + 1]
    gathered = jnp.sum(total, axis=0, keepdims=True)
    nu = NU_BASE + (EFACES * eps + gathered) / (2.0 * EFACES)
    top = tops[0]
    for g in range(1, N_GROUP):
        top = jnp.maximum(top, tops[g])
    peak = jnp.max(jnp.where(iota((1, LANES), 1) == LANES - 1, top, 0.0), axis=1, keepdims=True)
    square = iota((MODES, MODES), 0) == iota((MODES, MODES), 1)
    eigs = jnp.sum(jnp.where(square, eigs_ref[...], 0.0), axis=1, keepdims=True)
    coef = 1.0 / (mass[...] * (1.0 + speed / peak + nu * eigs))
    coef_ref[...] = coef

    condense_blocks(coef_ref, products, parts_a, pay_b)
    for c in range(N_Y):
        y = lax.rem(my_y + Y_ORDER[c], N_Y)
        rows[...] = pick(slot_hot[y], parts_a[...])

        def send_whole(n, carry):
            z = lax.rem(my_z + ring_offset(n), N_Z)
            q = y * N_Z + z
            whole_out[q] = rows[pl.ds(z, CAP, stride=16), :]
            remote(whole_out.at[q], whole_in.at[me], send_d, recv_d.at[c], {"dom": q}).start()
            return carry

        lax.fori_loop(0, N_Z if Y_ORDER[c] else N_Z - 1, send_whole, 0)
        if Y_ORDER[c] == 0:
            whole_in[me] = rows[pl.ds(my_z, CAP, stride=16), :]
    weighted[...] = inner[...] * coef[None]
    condense_loads(weighted, coupling, faceres, pay_b)
    parts_b[...] = jnp.concatenate(split3(pay_b[...]), axis=0)
    for c in range(N_Y):
        y = lax.rem(my_y + Y_ORDER[c], N_Y)
        rows[...] = pick(slot_hot[y], parts_b[...])

        def send_rest(n, carry):
            z = lax.rem(my_z + ring_offset(n), N_Z)
            q = y * N_Z + z
            pack_rest(rows, z, rest_out, q)
            remote(rest_out.at[q], rest_in.at[me], send_e, recv_e.at[c], {"dom": q}).start()
            return carry

        lax.fori_loop(0, N_Z if Y_ORDER[c] else N_Z - 1, send_rest, 0)
        if Y_ORDER[c] == 0:
            pack_rest(rows, my_z, rest_in, me)

    def to_grid(joined, start, height):
        for chunk in range(6):
            for n in range(height // 8):
                grid[start + n * 8 : start + n * 8 + 8, chunk, :] = joined[
                    n * 8 : n * 8 + 8, chunk * LANES : (chunk + 1) * LANES
                ]

    for c in range(N_Y):
        y = lax.rem(my_y + N_Y - Y_ORDER[c], N_Y)
        sources = pl.ds(0, N_Z if Y_ORDER[c] else N_Z - 1)
        remote(
            whole_out.at[sources], whole_in.at[sources], send_d, recv_d.at[c], following
        ).wait_recv()
        came = whole_in[pl.ds(pl.multiple_of(y * N_Z, N_Z), N_Z)].reshape(PART, LANES)
        stacked = jnp.concatenate(split3(jnp.transpose(came)), axis=0)
        found = dot(stacked, row_hot[y], NN)
        found = found[0:LANES] + found[LANES : 2 * LANES] + found[2 * LANES :]
        joined_a[...] = found if c == 0 else joined_a[...] + found
    to_grid(joined_a, 0, LANES)
    for c in range(N_Y):
        y = lax.rem(my_y + N_Y - Y_ORDER[c], N_Y)
        sources = pl.ds(0, N_Z if Y_ORDER[c] else N_Z - 1)
        remote(
            rest_out.at[sources], rest_in.at[sources], send_e, recv_e.at[c], following
        ).wait_recv()

        def take_rest(z, carry):
            unpack_rest(rest_in, y * N_Z + z, rows, z)
            return carry

        lax.fori_loop(0, N_Z, take_rest, 0, unroll=2)
        stacked = jnp.concatenate(split3(jnp.transpose(rows[...])[0:HALF]), axis=0)
        found = dot(stacked, row_hot[y], NN)
        found = found[0:HALF] + found[HALF : 2 * HALF] + found[2 * HALF :]
        joined_b[...] = found if c == 0 else joined_b[...] + found
    to_grid(joined_b, LANES, USED - LANES)
    first = face_ref[0:1, :]
    idle = jnp.concatenate(
        [first[:, chunk * LANES : (chunk + 1) * LANES] for chunk in range(6)]
        + [jnp.full((2, LANES), ROWS, I32)],
        axis=0,
    )
    idle = jnp.where(idle < ROWS, 0.0, 1.0)
    solved = solve_faces(grid, idle)
    for i in range(FNODES):
        for comp in range(COMPS):
            answer[comp * FNODES + i] = solved[i][comp]
    face_traces = jnp.concatenate([answer[:, chunk, :] for chunk in range(6)], axis=1)
    gap = jnp.zeros((LANES - COMPS * FNODES, FACES), BF16)
    high, low = split2(face_traces)
    both = jnp.concatenate([high, gap, low, gap], axis=0)

    for c in range(N_Y):
        y = lax.rem(my_y + Y_ORDER[c], N_Y)
        found = dot(row_hot[y], both, NT)
        rows[...] = found[:, 0:LANES] + found[:, LANES : 2 * LANES]

        def send_traces(n, carry):
            z = lax.rem(my_z + ring_offset(n), N_Z)
            p = y * N_Z + z
            pack_traces(rows, z, returning, p)
            remote(returning.at[p], back.at[me], send_f, recv_f.at[c], {"dom": p}).start()
            return carry

        lax.fori_loop(0, N_Z if Y_ORDER[c] else N_Z - 1, send_traces, 0)
        if Y_ORDER[c] == 0:
            pack_traces(rows, my_z, back, me)

    for c in range(N_Y):
        y = lax.rem(my_y + N_Y - Y_ORDER[c], N_Y)
        sources = pl.ds(0, N_Z if Y_ORDER[c] else N_Z - 1)
        remote(returning.at[sources], back.at[sources], send_f, recv_f.at[c], following).wait_recv()

        def take_traces(z, carry):
            unpack_traces(back, y * N_Z + z, rows, z)
            return carry

        lax.fori_loop(0, N_Z, take_traces, 0, unroll=2)
        turned = jnp.transpose(rows[...])[0 : COMPS * FNODES]
        stacked = jnp.concatenate(split2(turned), axis=0)
        found = dot(stacked, slot_hot[y], NN)
        found = found[0 : COMPS * FNODES] + found[COMPS * FNODES :]
        for comp in range(COMPS):
            for j in range(EFACES):
                piece = found[comp * FNODES : (comp + 1) * FNODES, j * LANES : (j + 1) * LANES]
                at = slice(j * FNODES, (j + 1) * FNODES)
                traces_ref[comp, at, :] = piece if c == 0 else traces_ref[comp, at, :] + piece
    remote(rest_out.at[others], rest_in.at[others], send_e, recv_e.at[0], following).wait_send()
    remote(returning.at[others], back.at[others], send_f, recv_f.at[0], following).wait_send()
    for leg in (first_leg, second_leg, top_leg):
        leg.wait_send()
    remote(whole_out.at[others], whole_in.at[others], send_d, recv_d.at[0], following).wait_send()


def update_kernel(traces_in, coef_ref, coupling_ref, inner_ref, update_ref, traces_ref):
    traces_ref[...] = traces_in[...]

    def substitute(k, carry):
        c = coupling_ref[k].astype(F32)
        coef = coef_ref[pl.ds(k, 1), :]
        for comp in range(COMPS):
            pulled = jnp.sum(c * traces_in[comp], axis=0, keepdims=True)
            update_ref[comp, pl.ds(k, 1), :] = coef * (inner_ref[comp, pl.ds(k, 1), :] - pulled)
        return carry

    lax.fori_loop(0, MODES, substitute, 0, unroll=8)


def local(
    density_modes,
    wave_speed,
    shock_flags,
    elem_mass,
    stiff_eigs,
    coupling,
    interior_res,
    face_res,
    send_rows,
    face_rows,
):
    vmem = pl.BlockSpec(memory_space=pltpu.VMEM)
    anywhere = pl.BlockSpec(memory_space=pltpu.HBM)
    dma = pltpu.SemaphoreType.DMA
    traces, coef = pl.pallas_call(
        step_kernel,
        out_shape=(
            pltpu.VMEM((COMPS, TRACE, LANES), F32),
            pltpu.VMEM((MODES, LANES), F32),
        ),
        in_specs=[anywhere] * 10,
        out_specs=(vmem, vmem),
        scratch_shapes=[
            pltpu.VMEM((MODES, LANES), F32),
            pltpu.VMEM((1, LANES), F32),
            pltpu.VMEM((1, LANES), I32),
            pltpu.VMEM((1, LANES), F32),
            pltpu.VMEM((1, MODES), F32),
            pltpu.VMEM((12, LANES), I32),
            pltpu.VMEM((2, FACES), I32),
            pltpu.VMEM((MODES, TRACE, LANES), BF16),
            pltpu.VMEM((COMPS, MODES, LANES), F32),
            pltpu.VMEM((COMPS, TRACE, LANES), F32),
            pltpu.VMEM((N_DOM, LANES), I32),
            pltpu.VMEM((COMPS, MODES, LANES), F32),
            pltpu.VMEM((N_DOM, 1, LANES), F32),
            pltpu.VMEM((N_DOM, 1, LANES), F32),
            pltpu.VMEM((16, 1, LANES), F32),
            pltpu.VMEM((N_DOM, 1, LANES), F32),
            pltpu.VMEM((1, 1, LANES), F32),
            pltpu.VMEM((N_GROUP, 1, LANES), F32),
            pltpu.VMEM((N_Y, PART, SLOTS), BF16),
            pltpu.VMEM((N_Y, PART, FACES), BF16),
            pltpu.VMEM((EFACES, MODES, TRI, LANES), F32),
            pltpu.VMEM((CAP, N_DOM, LANES), F32),
            pltpu.VMEM((LANES, SLOTS), F32),
            pltpu.VMEM((3 * LANES, SLOTS), BF16),
            pltpu.VMEM((3 * LANES, SLOTS), BF16),
            pltpu.VMEM((PART, LANES), F32),
            pltpu.VMEM((N_DOM, CAP, LANES), F32),
            pltpu.VMEM((N_DOM, CAP, LANES), F32),
            pltpu.VMEM((N_DOM, REST_TILE, LANES), F32),
            pltpu.VMEM((N_DOM, REST_TILE, LANES), F32),
            pltpu.VMEM((LANES, FACES), F32),
            pltpu.VMEM((HALF, FACES), F32),
            pltpu.VMEM((USED, 8, LANES), F32),
            pltpu.VMEM((COMPS * FNODES, 8, LANES), F32),
            pltpu.VMEM((N_DOM, RET_TILE, LANES), F32),
            pltpu.VMEM((N_DOM, RET_TILE, LANES), F32),
            dma((10,)),
            dma,
            dma,
            dma,
            dma,
            dma,
            dma,
            dma,
            dma((N_Y,)),
            dma,
            dma((N_Y,)),
            dma,
            dma((N_Y,)),
        ],
        compiler_params=pltpu.CompilerParams(
            collective_id=0, has_side_effects=True, vmem_limit_bytes=VMEM_LIMIT
        ),
        name="newton_step",
    )(
        density_modes,
        wave_speed[None, :],
        shock_flags[None, :],
        elem_mass[None, :],
        stiff_eigs[None, :],
        send_rows.reshape(12, LANES),
        face_rows,
        coupling,
        interior_res,
        face_res,
    )
    return pl.pallas_call(
        update_kernel,
        out_shape=(
            jax.ShapeDtypeStruct((COMPS, MODES, LANES), F32),
            jax.ShapeDtypeStruct((COMPS, TRACE, LANES), F32),
        ),
        in_specs=[vmem] * 4,
        out_specs=(vmem, vmem),
        compiler_params=pltpu.CompilerParams(vmem_limit_bytes=16 * 1024 * 1024),
        name="back_substitute",
    )(traces, coef, coupling, interior_res)


def solution(mesh):
    return jax.shard_map(
        local,
        mesh=mesh,
        in_specs=(
            P(None, ("group", "dom")),
            P(("group", "dom")),
            P(("group", "dom")),
            P(("group", "dom")),
            P(),
            P(None, None, ("group", "dom")),
            P(None, None, ("group", "dom")),
            P(None, None, ("group", "dom")),
            P(("group", "dom")),
            P(None, ("group", "dom")),
        ),
        out_specs=(P(None, None, ("group", "dom")), P(None, None, ("group", "dom"))),
        check_vma=False,
    )
```
